512 devices in a mesh: label: 64 (over x, z), fsdp: 8 (over y, core).
Axes of the slice: x: 4, y: 4, z: 16, core: 2. Of those that a mesh axis runs over, the one named last changes fastest.
Arguments:
- final_hidden: bfloat16 [64, 128, 3584], P('label', 'fsdp'), may hold values from -6 to 6
- norm_gain: float32 [3584], replicated, may hold values from 0.5 to 1.5
- label_weights: bfloat16 [64, 128, 3584], P('label'), may hold values from -0.09375 to 0.09375
- active_blocks: int32 [64, 64, 8], P('label', 'fsdp'), may hold values from 0 to 63, all different within a row; in each aligned block of 8 rows (0 to 7, 8 to 15, ..., all dimensions but the last counted through in order) at most 2 rows name the same one
- positives: int32 [64, 128, 8], P('label', 'fsdp'), may hold values from 0 to 1023
- gate_pre: bfloat16 [64, 128, 18944], P(None, 'fsdp', 'label'), may hold values from -6 to 6
- up_pre: bfloat16 [64, 128, 18944], P(None, 'fsdp', 'label'), may hold values from -6 to 6
- down_weight: bfloat16 [3584, 18944], P('fsdp', 'label'), may hold values from -0.046875 to 0.046875
Outputs:
- resid_grad: bfloat16 [64, 128, 3584], P('label', 'fsdp')
- down_grad: float32 [3584, 18944], P('fsdp', 'label')
- gate_grad: bfloat16 [64, 128, 18944], P(None, 'fsdp', 'label')
- up_grad: bfloat16 [64, 128, 18944], P(None, 'fsdp', 'label')
The draws below stay inside these ranges and needn't reach their ends.
Inputs may be any that keep to these rules, and one draw needn't show every extreme that they name: `active_blocks`: each query block names 8 different owners; among the 8 query blocks held by one device no owner is named more than 2 times. `positives`: A code k * 128 + j names label j of the k-th active block of the query's block.
All inputs are finite; a program needn't handle non-finite values.
Results may differ from the reference program's by a relative error of at most 0.017.
Values may be sent and summed in bfloat16 or wider, within the bound.
A program may use at most 64 MiB of HBM per device.

```python
import math
import jax
import jax.numpy as jnp
import numpy as np
from jax import lax

D = 3584
FF = 18944
LBLOCK = 128
ACTIVE = 8
POS = 8
QBLOCK = 2
QDEV = 16
QBLOCKS_DEV = 8
CAP = 2
N_LABEL = 64
N_FSDP = 8


def touch_ends(array, rng, least, top_value):
    extent = array.shape
    spot = [jax.random.randint(jax.random.fold_in(rng, axis), (), 0, extent[axis]) for axis in range(len(extent))]
    array = array.at[tuple(spot)].set(least)
    longest = extent.index(max(extent))
    spot[longest] = (spot[longest] + 1) % extent[longest]
    return array.at[tuple(spot)].set(top_value)


def block_levels(stream_key, shape, cuts, least, top_value):
    gain = 1.0
    for dim, blocks in cuts:
        heights = jax.random.uniform(jax.random.fold_in(jax.random.fold_in(stream_key, 6), dim), (blocks,), jnp.float32, least / len(cuts), top_value / len(cuts))
        gain = gain * jnp.repeat(jnp.exp(heights), shape[dim] // blocks).reshape((-1,) + (1,) * (len(shape) - 1 - dim))
    return gain


def assign_block(own_key, own, number, rows, number_of, top, limit, skew):
    sequence = jax.random.permutation(own_key, number_of)
    crowded, usual = shares(number_of, rows * top, limit, skew, True), shares(number_of, rows * top, limit, skew, False)
    places = jnp.arange(number_of)

    def named(lengths, offset_by):
        used = int((lengths > 0).sum())
        fixed = max(1, used // 4)
        shifted = fixed + (places - fixed + offset_by * (used - fixed)) % max(1, number_of - fixed)
        return jnp.zeros((number_of,), jnp.int32).at[sequence[jnp.where(places < fixed, places, shifted)]].set(jnp.asarray(lengths, jnp.int32))

    lengths = jnp.where(number % 4 == 0, named(crowded, number // 4), named(usual, number - number // 4 - 1))
    mixed = jax.random.permutation(jax.random.fold_in(own, 3), number_of)
    giver, taker = mixed[0:number_of // 2 * 2:2], mixed[1:number_of // 2 * 2:2]
    room = jnp.minimum(lengths[giver] - 1, limit - lengths[taker]) // 2
    room = jnp.where((giver == sequence[0]) | (taker == sequence[0]) | (lengths[taker] == 0), 0, jnp.maximum(room, 0))
    shifted = jax.random.randint(jax.random.fold_in(own, 4), (number_of // 2,), 0, 1 << 20) % (room + 1)
    lengths = lengths.at[giver].add(-shifted).at[taker].add(shifted)
    items = jnp.searchsorted(jnp.cumsum(lengths), jnp.arange(rows * top), side="right").astype(jnp.int32)
    listing = items.reshape(top, rows).T
    listing = listing[jax.random.permutation(jax.random.fold_in(own, 1), rows)]
    offset_by = jax.random.randint(jax.random.fold_in(own, 2), (rows, 1), 0, top)
    return jnp.take_along_axis(listing, (jnp.arange(top)[None, :] + offset_by) % top, axis=1)


def shares(number_of, total, limit, lean, full):
    loads = [(1 << 20) // math.isqrt(rank ** lean) + 1 for rank in range(1, number_of + 1)]
    largest = limit if full else min(limit, max(-(-total // number_of), total * loads[0] // sum(loads)))
    least = 1 if total - largest >= number_of - 1 else 0
    given, surplus = [largest] + [least] * (number_of - 1), total - largest - least * (number_of - 1)
    while surplus > 0:
        free = [i for i in range(1, number_of) if given[i] < largest] or [i for i in range(1, number_of) if given[i] < limit]
        mass, remaining = sum([loads[i] for i in free]), surplus
        for i in free:
            addition = min(limit - given[i], max(1, remaining * loads[i] // mass), surplus)
            given[i] = given[i] + addition
            surplus = surplus - addition
    return np.array(given)


def centred(rng, dims, spread, bound, cuts=(), kind=jnp.bfloat16):
    level = block_levels(rng, dims, cuts, -0.22, 0.18) if cuts else 1.0
    array = jax.random.normal(rng, dims, jnp.float32) * spread * level
    return jnp.minimum(jnp.maximum(array, -bound), bound).astype(kind)


def setup_inputs(seed: int = 0) -> dict:
    key_of = jax.random.split(jax.random.key(seed), 9)
    final_hidden = centred(key_of[0], (N_LABEL, N_FSDP * QDEV, D), 1.0, 6.0, ((0, 64), (1, 8)))
    norm_gain = jnp.clip(1.0 + 0.1 * jax.random.normal(key_of[1], (D,), jnp.float32), 0.5, 1.5)
    label_weights = centred(key_of[2], (N_LABEL, LBLOCK, D), D ** -0.5, 0.09375, ((0, 64),))
    active_blocks_keys = jax.random.split(jax.random.fold_in(key_of[3], 1), N_LABEL * (N_FSDP * QBLOCKS_DEV) // QBLOCKS_DEV)
    active_blocks_turns = jax.random.permutation(jax.random.fold_in(key_of[3], 3), N_LABEL * (N_FSDP * QBLOCKS_DEV) // QBLOCKS_DEV)
    active_blocks = jax.vmap(lambda own, number: assign_block(jax.random.fold_in(key_of[3], 2), own, number, QBLOCKS_DEV, N_LABEL, ACTIVE, CAP, 2))(active_blocks_keys, active_blocks_turns).reshape((N_LABEL, N_FSDP * QBLOCKS_DEV, ACTIVE))
    positives = touch_ends(jax.random.randint(key_of[4], (N_LABEL, N_FSDP * QDEV, POS), 0, ACTIVE * LBLOCK), jax.random.fold_in(key_of[4], 1), 0, (ACTIVE * LBLOCK) - 1).astype(jnp.int32)
    gate_pre = centred(key_of[5], (N_LABEL, N_FSDP * QDEV, FF), 1.0, 6.0, ((1, 8), (2, 64)))
    up_pre = centred(key_of[6], (N_LABEL, N_FSDP * QDEV, FF), 1.0, 6.0, ((1, 8), (2, 64)))
    down_weight = centred(key_of[7], (D, FF), FF ** -0.5, 0.046875, ((0, 8), (1, 64)))
    return dict(final_hidden=final_hidden, norm_gain=norm_gain, label_weights=label_weights, active_blocks=active_blocks, positives=positives, gate_pre=gate_pre, up_pre=up_pre, down_weight=down_weight)


norm_epsilon = 1e-06

def reference(final_hidden, norm_gain, label_weights, active_blocks, positives, gate_pre, up_pre, down_weight):
    query_total = final_hidden.shape[0] * final_hidden.shape[1]
    hidden_rows = final_hidden.reshape(query_total, D).astype(jnp.float32)
    inverse_rms = lax.rsqrt(lax.optimization_barrier(jnp.mean(hidden_rows * hidden_rows, axis=1, keepdims=True)) + norm_epsilon)
    normed = hidden_rows * inverse_rms
    embedded = (normed * norm_gain).astype(jnp.bfloat16)
    block_total = query_total // QBLOCK
    embed_blocks = embedded.reshape(block_total, QBLOCK, D)
    owner_table = active_blocks.reshape(block_total, ACTIVE)
    code_table = positives.reshape(block_total, QBLOCK, POS)
    targets = (jnp.arange(ACTIVE, dtype=jnp.int32)[:, None] * LBLOCK + jnp.arange(LBLOCK, dtype=jnp.int32)[None, :]).astype(jnp.int32)

    def one_block(item):
        block_embed, block_owners, block_codes = item
        weights_here = label_weights[block_owners].astype(jnp.float32)
        scores = jnp.einsum('qd,kld->kql', block_embed.astype(jnp.float32), weights_here)
        positive = jnp.any(block_codes[None, :, :, None] == targets[:, None, None, :], axis=2)
        target_sign = jnp.where(positive, 1.0, -1.0).astype(jnp.float32)
        margin = jnp.maximum(1.0 - target_sign * scores, 0.0)
        slope = (-2.0 * target_sign * margin).astype(jnp.bfloat16)
        slope = lax.optimization_barrier(slope).astype(jnp.float32)
        parts = jnp.einsum('kql,kld->kqd', slope, weights_here).astype(jnp.bfloat16)
        parts = lax.optimization_barrier(parts).astype(jnp.float32)
        return lax.optimization_barrier(jnp.sum(parts, axis=0))
    embed_grad = lax.map(one_block, (embed_blocks, owner_table, code_table)).reshape(query_total, D)
    scaled = norm_gain * embed_grad
    resid = inverse_rms * (scaled - normed * lax.optimization_barrier(jnp.mean(normed * scaled, axis=1, keepdims=True)))
    resid_bf = resid.astype(jnp.bfloat16)
    resid_grad = resid_bf.reshape(final_hidden.shape)
    gate_full = gate_pre.astype(jnp.float32)
    up_full = up_pre.astype(jnp.float32)
    sigma = jax.nn.sigmoid(gate_full)
    hidden_act = (gate_full * sigma * up_full).astype(jnp.bfloat16)
    label_count = gate_pre.shape[0]
    group_count = final_hidden.shape[1] // QDEV
    resid_groups = jnp.transpose(resid_bf.reshape(label_count, group_count, QDEV, D), (1, 0, 2, 3)).reshape(group_count, label_count * QDEV, D)
    hidden_groups = jnp.transpose(hidden_act.reshape(label_count, group_count, QDEV, FF), (1, 0, 2, 3)).reshape(group_count, label_count * QDEV, FF)

    def add_group(total, pair):
        group_resid, group_hidden = pair
        term = jnp.dot(group_resid.T, group_hidden, preferred_element_type=jnp.float32).astype(jnp.bfloat16)
        term = lax.optimization_barrier(term).astype(jnp.float32)
        return (total + term, None)
    down_grad, _ = lax.scan(add_group, jnp.zeros((D, FF), jnp.float32), (resid_groups, hidden_groups))
    hidden_grad = jnp.dot(resid_bf, down_weight, preferred_element_type=jnp.float32).reshape(gate_pre.shape)
    up_grad = (hidden_grad * gate_full * sigma).astype(jnp.bfloat16)
    gate_grad = (hidden_grad * up_full * sigma * (1.0 + gate_full * (1.0 - sigma))).astype(jnp.bfloat16)
    return (resid_grad, down_grad, gate_grad, up_grad)
```

```python
import functools

import jax
import jax.numpy as jnp
from jax import lax
from jax.experimental import pallas as pl
from jax.experimental.pallas import tpu as pltpu
from jax.sharding import PartitionSpec as P

LBLOCK = 128
ACTIVE = 8
POS = 8
QBLOCK = 2
NX = 4
LANES = 128
SPLIT = 18 * LANES

MESH = pl.DeviceIdType.MESH
norm_epsilon = 1e-06


def place(nz):
    me = lax.axis_index("label")
    other = lax.axis_index("fsdp")
    x = me // nz
    z = me % nz

    def device(px, pz):
        return (px * nz + pz, other)

    return x, z, device


def greet(devices):
    barrier = pltpu.get_barrier_semaphore()
    for target in devices:
        pl.semaphore_signal(barrier, inc=1, device_id=target, device_id_type=MESH)
    pl.semaphore_wait(barrier, len(devices))


def remote(src, dst, sems, slot, target):
    return pltpu.make_async_remote_copy(
        src_ref=src,
        dst_ref=dst,
        send_sem=sems[0].at[slot],
        recv_sem=sems[1].at[slot],
        device_id=target,
        device_id_type=MESH,
    )


def gather_kernel(nz, cut, own, out, *sems):
    local = sems[0]
    pair = [(sems[1 + 2 * i], sems[2 + 2 * i]) for i in range((len(sems) - 1) // 2)]
    zar, zal, zbr, zbl, xal, xar, fal, far, xb = pair
    half = nz // 2
    wide = own.shape[1]
    first, second = pl.ds(0, cut), pl.ds(cut, wide - cut)
    low, high = pl.ds(0, cut // 2), pl.ds(cut // 2, cut // 2)
    x, z, device = place(nz)
    xp, xm, xo = (x + 1) % NX, (x + NX - 1) % NX, (x + 2) % NX
    zp, zm = (z + 1) % nz, (z + nz - 1) % nz
    to_xp, to_xm, to_xo = device(xp, z), device(xm, z), device(xo, z)
    to_zp, to_zm = device(x, zp), device(x, zm)

    def block(sx, sz, columns):
        return out.at[sx, sz, :, columns]

    def move(sx, sz, columns, sem, slot, target):
        there = block(sx, sz, columns)
        return remote(there, there, sem, slot, target)

    def bundle(sz, sem, slot, target):
        there = out.at[:, sz, :, second]
        return remote(there, there, sem, slot, target)

    def spread(sz):
        move(x, sz, first, xal, sz, to_xp).start()
        move(x, sz, first, xar, sz, to_xm).start()

    def pass_on(sz):
        move(xm, sz, first, xal, sz, to_xp).wait_recv()
        move(xm, sz, low, fal, sz, to_xp).start()
        move(xp, sz, first, xar, sz, to_xm).wait_recv()
        move(xp, sz, high, far, sz, to_xm).start()

    keep = pltpu.make_async_copy(own, out.at[x, z], local)
    keep.start()
    keep.wait()
    greet((to_xp, to_xm, to_xo, to_zp, to_zm))
    move(x, z, second, xb, 0, to_xp).start()
    move(x, z, second, xb, 1, to_xm).start()
    move(x, z, second, xb, 2, to_xo).start()
    move(x, z, first, zar, 0, to_zp).start()
    move(x, z, first, zal, 0, to_zm).start()
    spread(z)
    move(xm, z, second, xb, 0, to_xp).wait_recv()
    move(xp, z, second, xb, 1, to_xm).wait_recv()
    move(xo, z, second, xb, 2, to_xo).wait_recv()
    bundle(z, zbr, 0, to_zp).start()
    bundle(z, zbl, 0, to_zm).start()

    def step(s, carry):
        back, ahead = (z + nz - s) % nz, (z + s) % nz
        move(x, back, first, zar, s - 1, to_zp).wait_recv()
        move(x, back, first, zar, s, to_zp).start()
        move(x, ahead, first, zal, s - 1, to_zm).wait_recv()

        @pl.when(s < half - 1)
        def _():
            move(x, ahead, first, zal, s, to_zm).start()

        spread(back)
        spread(ahead)
        bundle(back, zbr, s - 1, to_zp).wait_recv()

        @pl.when(s < half - 1)
        def _():
            bundle(back, zbr, s, to_zp).start()

        bundle(ahead, zbl, s - 1, to_zm).wait_recv()
        bundle(ahead, zbl, s, to_zm).start()
        pass_on((back + 1) % nz)

        @pl.when(s > 1)
        def _():
            pass_on((ahead + nz - 1) % nz)

        return carry

    lax.fori_loop(1, half, step, 0)
    far_z = (z + half) % nz
    move(x, far_z, first, zar, half - 1, to_zp).wait_recv()
    spread(far_z)
    pass_on((far_z + 1) % nz)
    pass_on((far_z + nz - 1) % nz)
    pass_on(far_z)
    bundle(far_z, zbl, half - 1, to_zm).wait_recv()

    def finish(i, carry):
        move(xo, i, low, fal, i, to_xp).wait_recv()
        move(xo, i, high, far, i, to_xm).wait_recv()
        move(x, i, first, xal, i, to_xp).wait_send()
        move(x, i, first, xar, i, to_xm).wait_send()
        move(xm, i, low, fal, i, to_xp).wait_send()
        move(xp, i, high, far, i, to_xm).wait_send()
        return carry

    lax.fori_loop(0, nz, finish, 0)
    for slot, target in enumerate((to_xp, to_xm, to_xo)):
        move(x, z, second, xb, slot, target).wait_send()

    def drain(s, carry):
        move(x, z, first, zar, s, to_zp).wait_send()
        bundle(z, zbl, s, to_zm).wait_send()

        @pl.when(s < half - 1)
        def _():
            move(x, z, first, zal, s, to_zm).wait_send()
            bundle(z, zbr, s, to_zp).wait_send()

        return carry

    lax.fori_loop(0, half, drain, 0)


def pairs_of(counts):
    return [pltpu.SemaphoreType.DMA((n,)) for n in counts for _ in range(2)]


def gather_rows(own, nz, cut, number):
    rows, wide = own.shape
    half = nz // 2
    return pl.pallas_call(
        functools.partial(gather_kernel, nz, cut),
        out_shape=jax.ShapeDtypeStruct((NX, nz, rows, wide), own.dtype),
        in_specs=[pl.BlockSpec(memory_space=pltpu.VMEM)],
        out_specs=pl.BlockSpec(memory_space=pltpu.VMEM),
        scratch_shapes=[
            pltpu.SemaphoreType.DMA,
            *pairs_of((half, half - 1, half - 1, half, nz, nz, nz, nz, 3)),
        ],
        compiler_params=pltpu.CompilerParams(
            collective_id=number, has_side_effects=True, vmem_limit_bytes=24 << 20
        ),
        cost_estimate=pl.CostEstimate(flops=0, bytes_accessed=150 << 20, transcendentals=0),
    )(own)


def scatter_kernel(nz, cut, mine, out, hl, hr, sr, sl, fl, fr, y, zr, zl, br, bl, q, xr, *sems):
    pair = [(sems[2 * i], sems[2 * i + 1]) for i in range(len(sems) // 2)]
    shl, shr, sfl, sfr, szr, szl, sbr, sbl, sxb = pair
    half = nz // 2
    wide = out.shape[1]
    first, second = pl.ds(0, cut), pl.ds(cut, wide - cut)
    low, high = pl.ds(0, cut // 2), pl.ds(cut // 2, cut // 2)
    x, z, device = place(nz)
    xp, xm, xo = (x + 1) % NX, (x + NX - 1) % NX, (x + 2) % NX
    zp, zm = (z + 1) % nz, (z + nz - 1) % nz
    to_xp, to_xm, to_xo = device(xp, z), device(xm, z), device(xo, z)
    to_zp, to_zm = device(x, zp), device(x, zm)

    def far_right(t):
        return remote(mine.at[xo, t, :, low], hl.at[t], shl, t, to_xp)

    def far_left(t):
        return remote(mine.at[xo, t, :, high], hr.at[t], shr, t, to_xm)

    def near_right(t):
        return remote(sr.at[t], fl.at[t], sfl, t, to_xp)

    def near_left(t):
        return remote(sl.at[t], fr.at[t], sfr, t, to_xm)

    def opens(t):
        far_right(t).start()
        far_left(t).start()

    def joins(t):
        far_right(t).wait_recv()
        sr[t, :, low] = mine[xp, t, :, low] + hl[t]
        sr[t, :, high] = mine[xp, t, :, high]
        near_right(t).start()
        far_left(t).wait_recv()
        sl[t, :, high] = mine[xm, t, :, high] + hr[t]
        sl[t, :, low] = mine[xm, t, :, low]
        near_left(t).start()

    def sums(t):
        near_right(t).wait_recv()
        near_left(t).wait_recv()
        total = mine[x, t, :, first].astype(jnp.float32) + fl[t].astype(jnp.float32)
        y[t] = (total + fr[t].astype(jnp.float32)).astype(y.dtype)

    def ahead(s):
        return (z + half + 1 - s) % nz

    def back(s):
        return (z + nz - half - 1 + s) % nz

    def chain_right(s):
        return remote(zr.at[s - 2], zr.at[s - 1], szr, s - 1, to_zp)

    def chain_left(s):
        return remote(zl.at[s - 3], zl.at[s - 2], szl, s - 2, to_zm)

    def wide_right(s):
        return remote(br.at[s - 3], br.at[s - 2], sbr, s - 2, to_zp)

    def wide_left(s):
        return remote(bl.at[s - 2], bl.at[s - 1], sbl, s - 1, to_zm)

    start_right = remote(y.at[ahead(1)], zr.at[0], szr, 0, to_zp)
    start_left = remote(y.at[back(2)], zl.at[0], szl, 0, to_zm)
    start_wide_left = remote(mine.at[:, back(1), :, second], bl.at[0], sbl, 0, to_zm)
    start_wide_right = remote(mine.at[:, ahead(2), :, second], br.at[0], sbr, 0, to_zp)

    greet((to_xp, to_xm, to_xo, to_zp, to_zm))
    start_wide_left.start()
    start_wide_right.start()
    opens(ahead(1))
    opens(ahead(2))
    opens(back(2))
    opens(ahead(3))
    opens(back(3))
    joins(ahead(1))
    joins(ahead(2))
    joins(back(2))
    sums(ahead(1))
    start_right.start()

    def step(s, carry):
        @pl.when(s < half - 1)
        def _():
            opens(ahead(s + 2))
            opens(back(s + 2))

        @pl.when(s == half - 1)
        def _():
            opens(z)

        @pl.when(s < half)
        def _():
            joins(ahead(s + 1))
            joins(back(s + 1))

        @pl.when(s == half)
        def _():
            joins(z)

        sums(ahead(s))
        sums(back(s))

        @pl.when(s == 2)
        def _():
            start_left.start()

        remote(zr.at[s - 2], zr.at[s - 2], szr, s - 2, to_zp).wait_recv()
        zr[s - 2] = zr[s - 2] + y[ahead(s)]
        chain_right(s).start()

        @pl.when(s > 2)
        def _():
            remote(zl.at[s - 3], zl.at[s - 3], szl, s - 3, to_zm).wait_recv()
            zl[s - 3] = zl[s - 3] + y[back(s)]
            chain_left(s).start()

        remote(bl.at[s - 2], bl.at[s - 2], sbl, s - 2, to_zm).wait_recv()
        bl[s - 2] = bl[s - 2] + mine[:, back(s), :, second]
        wide_left(s).start()

        @pl.when(s > 2)
        def _():
            remote(br.at[s - 3], br.at[s - 3], sbr, s - 3, to_zp).wait_recv()
            br[s - 3] = br[s - 3] + mine[:, ahead(s), :, second]
            wide_right(s).start()

        return carry

    lax.fori_loop(2, half + 1, step, 0)
    remote(bl.at[half - 1], bl.at[half - 1], sbl, half - 1, to_zm).wait_recv()
    remote(br.at[half - 2], br.at[half - 2], sbr, half - 2, to_zp).wait_recv()
    q[...] = (bl[half - 1] + br[half - 2]) + mine[:, z, :, second]
    near = ((xp, to_xp), (xm, to_xm), (xo, to_xo))
    for slot, (px, target) in enumerate(near):
        remote(q.at[px], xr.at[slot], sxb, slot, target).start()
    sums(z)
    remote(zr.at[half - 1], zr.at[half - 1], szr, half - 1, to_zp).wait_recv()
    remote(zl.at[half - 2], zl.at[half - 2], szl, half - 2, to_zm).wait_recv()
    total = y[z].astype(jnp.float32) + zr[half - 1].astype(jnp.float32)
    out[:, first] = total + zl[half - 2].astype(jnp.float32)
    for slot, (px, target) in enumerate(near):
        remote(q.at[px], xr.at[slot], sxb, slot, target).wait_recv()
    rest = q[x].astype(jnp.float32) + xr[0].astype(jnp.float32)
    out[:, second] = rest + xr[1].astype(jnp.float32) + xr[2].astype(jnp.float32)
    for slot, (px, target) in enumerate(near):
        remote(q.at[px], xr.at[slot], sxb, slot, target).wait_send()

    def finish(t, carry):
        far_right(t).wait_send()
        far_left(t).wait_send()
        near_right(t).wait_send()
        near_left(t).wait_send()
        return carry

    lax.fori_loop(0, nz, finish, 0)

    def drain(s, carry):
        remote(zr.at[s], zr.at[s], szr, s, to_zp).wait_send()
        remote(bl.at[s], bl.at[s], sbl, s, to_zm).wait_send()

        @pl.when(s < half - 1)
        def _():
            remote(zl.at[s], zl.at[s], szl, s, to_zm).wait_send()
            remote(br.at[s], br.at[s], sbr, s, to_zp).wait_send()

        return carry

    lax.fori_loop(0, half, drain, 0)


def scatter_rows(mine, cut, number):
    _, nz, rows, wide = mine.shape
    half = nz // 2
    rest = wide - cut
    kind = mine.dtype
    return pl.pallas_call(
        functools.partial(scatter_kernel, nz, cut),
        out_shape=jax.ShapeDtypeStruct((rows, wide), jnp.float32),
        in_specs=[pl.BlockSpec(memory_space=pltpu.VMEM)],
        out_specs=pl.BlockSpec(memory_space=pltpu.VMEM),
        scratch_shapes=[
            pltpu.VMEM((nz, rows, cut // 2), kind),
            pltpu.VMEM((nz, rows, cut // 2), kind),
            *[pltpu.VMEM((nz, rows, cut), kind)] * 5,
            pltpu.VMEM((half, rows, cut), kind),
            pltpu.VMEM((half - 1, rows, cut), kind),
            pltpu.VMEM((half - 1, NX, rows, rest), kind),
            pltpu.VMEM((half, NX, rows, rest), kind),
            pltpu.VMEM((NX, rows, rest), kind),
            pltpu.VMEM((3, rows, rest), kind),
            *pairs_of((nz, nz, nz, nz, half, half - 1, half - 1, half, 3)),
        ],
        compiler_params=pltpu.CompilerParams(
            collective_id=number, has_side_effects=True, vmem_limit_bytes=40 << 20
        ),
        cost_estimate=pl.CostEstimate(flops=0, bytes_accessed=150 << 20, transcendentals=0),
    )(mine)


def shards(
    final_hidden, norm_gain, label_weights, active_blocks, positives, gate_pre, up_pre, down_weight
):
    owners = lax.axis_size("label")
    nz = owners // NX
    hidden_rows = final_hidden[0].astype(jnp.float32)
    query_count, width = hidden_rows.shape
    block_count = query_count // QBLOCK
    down_full = lax.all_gather(down_weight, "fsdp", axis=0, tiled=True)
    inverse_rms = lax.rsqrt(
        jnp.mean(hidden_rows * hidden_rows, axis=1, keepdims=True) + norm_epsilon
    )
    normed = hidden_rows * inverse_rms
    embedded = (normed * norm_gain).astype(jnp.bfloat16)
    named = jnp.broadcast_to(
        active_blocks[0][:, None, :], (block_count, QBLOCK, ACTIVE)
    ).reshape(query_count, ACTIVE)
    codes = positives[0]
    marks = jnp.concatenate([named, codes // LBLOCK, codes % LBLOCK], axis=1)
    marks = jnp.pad(marks, ((0, 0), (0, LANES - marks.shape[1]))).astype(jnp.bfloat16)
    rows = gather_rows(jnp.concatenate([embedded, marks], axis=1), nz, SPLIT, 0)
    rows = rows.reshape(owners * query_count, width + LANES)
    label_rows = label_weights[0]
    label_wide = jnp.pad(label_rows, ((0, 0), (0, LANES)))
    scores = lax.dot_general(
        rows, label_wide, (((1,), (1,)), ((), ())), preferred_element_type=jnp.float32
    )
    marks = rows[:, width:].astype(jnp.int32)
    me = lax.axis_index("label")
    hit = marks[:, :ACTIVE] == me
    named_here = jnp.any(hit, axis=1, keepdims=True)
    spot = jnp.sum(
        jnp.where(hit, jnp.arange(ACTIVE, dtype=jnp.int32), 0), axis=1, keepdims=True
    )
    label_of = jnp.where(
        marks[:, ACTIVE : ACTIVE + POS] == spot, marks[:, ACTIVE + POS : ACTIVE + 2 * POS], -1
    )
    labels_here = jnp.arange(LBLOCK, dtype=jnp.int32)[None, :]
    positive = label_of[:, 0:1] == labels_here
    for p in range(1, POS):
        positive = positive | (label_of[:, p : p + 1] == labels_here)
    target_sign = jnp.where(positive, 1.0, -1.0)
    margin = jnp.maximum(1.0 - target_sign * scores, 0.0)
    slope = jnp.where(named_here, -2.0 * target_sign * margin, 0.0).astype(jnp.bfloat16)
    part = jnp.dot(slope, label_rows, preferred_element_type=jnp.float32).astype(jnp.bfloat16)
    embed_grad = scatter_rows(part.reshape(NX, nz, query_count, width), SPLIT, 1)
    scaled = norm_gain * embed_grad
    resid = inverse_rms * (scaled - normed * jnp.mean(normed * scaled, axis=1, keepdims=True))
    resid_bf = resid.astype(jnp.bfloat16)
    row_grads = gather_rows(resid_bf, nz, SPLIT, 2).reshape(owners * query_count, width)
    gate_full = gate_pre.astype(jnp.float32)
    up_full = up_pre.astype(jnp.float32)
    sigma = jax.nn.sigmoid(gate_full)
    ff_local = gate_pre.shape[2]
    hidden_act = (gate_full * sigma * up_full).astype(jnp.bfloat16)
    hidden_act = hidden_act.reshape(owners * query_count, ff_local)
    hidden_grad = jnp.dot(row_grads, down_full, preferred_element_type=jnp.float32)
    down_grad = lax.psum_scatter(
        lax.dot_general(
            row_grads, hidden_act, (((0,), (0,)), ((), ())), preferred_element_type=jnp.float32
        ).astype(jnp.bfloat16),
        "fsdp",
        scatter_dimension=0,
        tiled=True,
    ).astype(jnp.float32)
    hidden_grad = hidden_grad.reshape(gate_pre.shape)
    up_grad = (hidden_grad * gate_full * sigma).astype(jnp.bfloat16)
    gate_grad = (hidden_grad * up_full * sigma * (1.0 + gate_full * (1.0 - sigma))).astype(
        jnp.bfloat16
    )
    return (resid_bf[None], down_grad, gate_grad, up_grad)


def solution(mesh):
    placed = (
        P("label", "fsdp", None),
        P(),
        P("label", None, None),
        P("label", "fsdp", None),
        P("label", "fsdp", None),
        P(None, "fsdp", "label"),
        P(None, "fsdp", "label"),
        P("fsdp", "label"),
    )
    return jax.shard_map(
        shards,
        mesh=mesh,
        in_specs=placed,
        out_specs=(
            P("label", "fsdp", None),
            P("fsdp", "label"),
            P(None, "fsdp", "label"),
            P(None, "fsdp", "label"),
        ),
        check_vma=False,
    )
```

```python
import functools

import jax
import jax.numpy as jnp
from jax import lax
from jax.experimental import pallas as pl
from jax.experimental.layout import Layout, with_layout_constraint
from jax.experimental.pallas import tpu as pltpu
from jax.sharding import PartitionSpec as P

LBLOCK = 128
ACTIVE = 8
POS = 8
QBLOCK = 2
NX = 4
NY = 4
CORES = 2
CAP = 2
GROUP = 4
CHUNK = 512
LANES = 128
SPLIT = 18 * LANES

MESH = pl.DeviceIdType.MESH
norm_epsilon = 1e-06


def place(nz):
    me = lax.axis_index("label")
    other = lax.axis_index("fsdp")
    x = me // nz
    z = me % nz

    def device(px, pz):
        return (px * nz + pz, other)

    return x, z, device


def greet(devices):
    barrier = pltpu.get_barrier_semaphore()
    for target in devices:
        pl.semaphore_signal(barrier, inc=1, device_id=target, device_id_type=MESH)
    pl.semaphore_wait(barrier, len(devices))


def remote(src, dst, sems, slot, target):
    return pltpu.make_async_remote_copy(
        src_ref=src,
        dst_ref=dst,
        send_sem=sems[0].at[slot],
        recv_sem=sems[1].at[slot],
        device_id=target,
        device_id_type=MESH,
    )


def gather_kernel(nz, cut, own, out, *sems):
    local = sems[0]
    pair = [(sems[1 + 2 * i], sems[2 + 2 * i]) for i in range((len(sems) - 1) // 2)]
    zar, zal, zbr, zbl, xal, xar, fal, far, xb = pair
    half = nz // 2
    wide = own.shape[1]
    first, second = pl.ds(0, cut), pl.ds(cut, wide - cut)
    low, high = pl.ds(0, cut // 2), pl.ds(cut // 2, cut // 2)
    x, z, device = place(nz)
    xp, xm, xo = (x + 1) % NX, (x + NX - 1) % NX, (x + 2) % NX
    zp, zm = (z + 1) % nz, (z + nz - 1) % nz
    to_xp, to_xm, to_xo = device(xp, z), device(xm, z), device(xo, z)
    to_zp, to_zm = device(x, zp), device(x, zm)

    def block(sx, sz, columns):
        return out.at[sx, sz, :, columns]

    def move(sx, sz, columns, sem, slot, target):
        there = block(sx, sz, columns)
        return remote(there, there, sem, slot, target)

    def bundle(sz, sem, slot, target):
        there = out.at[:, sz, :, second]
        return remote(there, there, sem, slot, target)

    def spread(sz):
        move(x, sz, first, xal, sz, to_xp).start()
        move(x, sz, first, xar, sz, to_xm).start()

    def pass_on(sz):
        move(xm, sz, first, xal, sz, to_xp).wait_recv()
        move(xm, sz, low, fal, sz, to_xp).start()
        move(xp, sz, first, xar, sz, to_xm).wait_recv()
        move(xp, sz, high, far, sz, to_xm).start()

    keep = pltpu.make_async_copy(own, out.at[x, z], local)
    keep.start()
    keep.wait()
    greet((to_xp, to_xm, to_xo, to_zp, to_zm))
    move(x, z, second, xb, 0, to_xp).start()
    move(x, z, second, xb, 1, to_xm).start()
    move(x, z, second, xb, 2, to_xo).start()
    move(x, z, first, zar, 0, to_zp).start()
    move(x, z, first, zal, 0, to_zm).start()
    spread(z)
    move(xm, z, second, xb, 0, to_xp).wait_recv()
    move(xp, z, second, xb, 1, to_xm).wait_recv()
    move(xo, z, second, xb, 2, to_xo).wait_recv()
    bundle(z, zbr, 0, to_zp).start()
    bundle(z, zbl, 0, to_zm).start()

    def step(s, carry):
        back, ahead = (z + nz - s) % nz, (z + s) % nz
        move(x, back, first, zar, s - 1, to_zp).wait_recv()
        move(x, back, first, zar, s, to_zp).start()
        move(x, ahead, first, zal, s - 1, to_zm).wait_recv()

        @pl.when(s < half - 1)
        def _():
            move(x, ahead, first, zal, s, to_zm).start()

        spread(back)
        spread(ahead)
        bundle(back, zbr, s - 1, to_zp).wait_recv()

        @pl.when(s < half - 1)
        def _():
            bundle(back, zbr, s, to_zp).start()

        bundle(ahead, zbl, s - 1, to_zm).wait_recv()
        bundle(ahead, zbl, s, to_zm).start()
        pass_on((back + 1) % nz)

        @pl.when(s > 1)
        def _():
            pass_on((ahead + nz - 1) % nz)

        return carry

    lax.fori_loop(1, half, step, 0)
    far_z = (z + half) % nz
    move(x, far_z, first, zar, half - 1, to_zp).wait_recv()
    spread(far_z)
    pass_on((far_z + 1) % nz)
    pass_on((far_z + nz - 1) % nz)
    pass_on(far_z)
    bundle(far_z, zbl, half - 1, to_zm).wait_recv()

    def finish(i, carry):
        move(xo, i, low, fal, i, to_xp).wait_recv()
        move(xo, i, high, far, i, to_xm).wait_recv()
        move(x, i, first, xal, i, to_xp).wait_send()
        move(x, i, first, xar, i, to_xm).wait_send()
        move(xm, i, low, fal, i, to_xp).wait_send()
        move(xp, i, high, far, i, to_xm).wait_send()
        return carry

    lax.fori_loop(0, nz, finish, 0)
    for slot, target in enumerate((to_xp, to_xm, to_xo)):
        move(x, z, second, xb, slot, target).wait_send()

    def drain(s, carry):
        move(x, z, first, zar, s, to_zp).wait_send()
        bundle(z, zbl, s, to_zm).wait_send()

        @pl.when(s < half - 1)
        def _():
            move(x, z, first, zal, s, to_zm).wait_send()
            bundle(z, zbr, s, to_zp).wait_send()

        return carry

    lax.fori_loop(0, half, drain, 0)


def pairs_of(counts):
    return [pltpu.SemaphoreType.DMA((n,)) for n in counts for _ in range(2)]


def gather_rows(own, nz, cut, number):
    rows, wide = own.shape
    half = nz // 2
    return pl.pallas_call(
        functools.partial(gather_kernel, nz, cut),
        out_shape=jax.ShapeDtypeStruct((NX, nz, rows, wide), own.dtype),
        in_specs=[pl.BlockSpec(memory_space=pltpu.VMEM)],
        out_specs=pl.BlockSpec(memory_space=pltpu.VMEM),
        scratch_shapes=[
            pltpu.SemaphoreType.DMA,
            *pairs_of((half, half - 1, half - 1, half, nz, nz, nz, nz, 3)),
        ],
        compiler_params=pltpu.CompilerParams(
            collective_id=number, has_side_effects=True, vmem_limit_bytes=24 << 20
        ),
        cost_estimate=pl.CostEstimate(flops=0, bytes_accessed=150 << 20, transcendentals=0),
    )(own)


def halves(wide):
    tiles = wide // LANES // 2 * LANES
    return pl.ds(0, tiles), pl.ds(tiles, wide - tiles)


class RingOfFour:
    def __init__(self, here, to_next, to_prev, sent, landed, passing, sems, wide):
        self.spots = ((here + 1) % 4, (here + 3) % 4, (here + 2) % 4)
        self.here, self.to_next, self.to_prev = here, to_next, to_prev
        self.sent, self.landed, self.passing, self.sems = sent, landed, passing, sems
        self.low, self.high = halves(wide)

    def copy(self, g, i):
        nxt, prv, opp = self.spots
        sent, landed, (over_next, over_prev) = self.sent, self.landed, self.passing
        low, high = self.low, self.high
        source, target = (
            (sent(g, nxt), landed(g, self.here)),
            (sent(g, prv), landed(g, self.here)),
            (sent(g, opp).at[:, low], over_next.at[g]),
            (sent(g, opp).at[:, high], over_prev.at[g]),
            (over_next.at[g], landed(g, prv).at[:, low]),
            (over_prev.at[g], landed(g, nxt).at[:, high]),
        )[i]
        return remote(source, target, self.sems[i], g, self.to_prev if i % 2 else self.to_next)

    def start(self, g):
        for i in (2, 3, 0, 1):
            self.copy(g, i).start()

    def pass_on(self, g):
        for i in (2, 3):
            self.copy(g, i).wait_recv()
            self.copy(g, i + 2).start()

    def arrive(self, g):
        for i in (0, 1, 4, 5):
            self.copy(g, i).wait_recv()

    def drain(self, g):
        for i in range(6):
            self.copy(g, i).wait_send()


def chunks(wide, body):
    def one(i, carry):
        body(pl.ds(pl.multiple_of(i * CHUNK, CHUNK), CHUNK))
        return carry

    lax.fori_loop(0, wide // CHUNK, one, 0)


def route_kernel(
    nz, own, label, out, zg, sel, got, slope, picks, part, back, u, zr, zl, t1, t2, t3, t4, *sems
):
    pair = [(sems[2 * i], sems[2 * i + 1]) for i in range(len(sems) // 2)]
    szr, szl, scr, scl = pair[:4]
    half, groups = nz // 2, nz // GROUP
    wide = out.shape[1]
    rows = own.shape[0]
    taken = GROUP * rows
    slots = CAP * QBLOCK
    x, z, device = place(nz)
    xp, xm, xo = (x + 1) % NX, (x + NX - 1) % NX, (x + 2) % NX
    to_xp, to_xm = device(xp, z), device(xm, z)
    to_zp, to_zm = device(x, (z + 1) % nz), device(x, (z + nz - 1) % nz)
    f32, bf16 = jnp.float32, jnp.bfloat16
    out_ring = RingOfFour(
        x, to_xp, to_xm, lambda g, d: sel.at[g, d], lambda g, d: got.at[g, d], (t1, t2), pair[4:10], own.shape[1]
    )
    back_ring = RingOfFour(
        x, to_xp, to_xm, lambda g, d: part.at[g, d], lambda g, d: back.at[g, d], (t3, t4), pair[10:16], wide
    )

    def right(s):
        source = own if s == 1 else zg.at[2 * s - 3]
        return remote(source, zg.at[2 * s - 1], szr, s - 1, to_zp)

    def left(s):
        source = own if s == 1 else zg.at[2 * s - 2]
        return remote(source, zg.at[2 * s], szl, s - 1, to_zm)

    def select(g):
        mine = pl.ds(GROUP * g, GROUP)
        marks = zg[mine, :, wide:].reshape(taken, LANES).astype(f32)
        row = lax.broadcasted_iota(jnp.int32, (taken, LANES), 0)
        col = lax.broadcasted_iota(jnp.int32, (taken, LANES), 1)
        owner = ((col // (GROUP * slots)) * nz + z).astype(f32)
        hit = marks[:, 0:1] == owner
        for k in range(1, ACTIVE):
            hit = hit | (marks[:, k : k + 1] == owner)
        before = lax.broadcasted_iota(jnp.int32, (taken, taken), 0)
        other = lax.broadcasted_iota(jnp.int32, (taken, taken), 1)
        earlier = (before // rows == other // rows) & (other // QBLOCK < before // QBLOCK)
        earlier = jnp.where(earlier & (other % QBLOCK == 0), 1.0, 0.0).astype(bf16)
        rank = jnp.dot(earlier, jnp.where(hit, 1.0, 0.0).astype(bf16), preferred_element_type=f32)
        slot = QBLOCK * rank + (row % QBLOCK).astype(f32)
        fits = (row // rows == (col // slots) % GROUP) & ((col % slots).astype(f32) == slot)
        pick = jnp.where(hit & fits, 1.0, 0.0).astype(bf16)
        picks[g] = pick
        wide_row = lax.broadcasted_iota(jnp.int32, (LANES, LANES), 0)
        wide_col = lax.broadcasted_iota(jnp.int32, (LANES, LANES), 1)
        unit = jnp.where(wide_row == wide_col, 1.0, 0.0).astype(bf16)
        turned = lax.dot_general(unit, pick, (((1,), (1,)), ((), ())), preferred_element_type=f32)
        turned = turned[: NX * GROUP * slots].astype(bf16)

        def place_columns(columns, count):
            block = zg[mine, :, columns].reshape(taken, count)
            made = jnp.dot(turned, block, preferred_element_type=f32).astype(bf16)
            sel[g, :, :, columns] = made.reshape(NX, GROUP * slots, count)

        chunks(wide, lambda columns: place_columns(columns, CHUNK))
        place_columns(pl.ds(wide, LANES), LANES)
        out_ring.start(g)
        got[g, x] = sel[g, x]

    def score(g):
        out_ring.arrive(g)
        count = NX * GROUP * slots
        block = got[g, :, :, :wide].reshape(count, wide)
        scores = lax.dot_general(
            block, label[...], (((1,), (1,)), ((), ())), preferred_element_type=f32
        )
        marks = got[g, :, :, wide:].reshape(count, LANES).astype(f32)
        me = (x * nz + z).astype(f32)
        spot = jnp.zeros((count, 1), f32)
        for k in range(1, ACTIVE):
            spot = spot + jnp.where(marks[:, k : k + 1] == me, float(k), 0.0)
        named = lax.broadcasted_iota(jnp.int32, (count, LBLOCK), 1).astype(f32)
        positive = jnp.zeros((count, LBLOCK), jnp.bool_)
        for p in range(ACTIVE, ACTIVE + POS):
            code = jnp.where(marks[:, p : p + 1] == spot, marks[:, p + POS : p + POS + 1], -1.0)
            positive = positive | (code == named)
        sign = jnp.where(positive, 1.0, -1.0)
        slope[g] = (-2.0 * sign * jnp.maximum(1.0 - sign * scores, 0.0)).astype(bf16)

    def give(g):
        steep = slope[g]

        def columns_of(columns):
            made = jnp.dot(steep, label[:, columns], preferred_element_type=f32).astype(bf16)
            part[g, :, :, columns] = made.reshape(NX, GROUP * slots, CHUNK)

        chunks(wide, columns_of)
        back_ring.start(g)
        back[g, x] = part[g, x]

    def unselect(g):
        back_ring.arrive(g)
        count = NX * GROUP * slots
        pick = picks[g][:, :count]

        def columns_of(columns):
            block = back[g, :, :, columns].reshape(count, CHUNK)
            made = jnp.dot(pick, block, preferred_element_type=f32).astype(bf16)
            u[pl.ds(GROUP * g, GROUP), :, columns] = made.reshape(GROUP, rows, CHUNK)

        chunks(wide, columns_of)

    def chain_right(s):
        source = u.at[nz - 1] if s == 1 else zr.at[s - 2]
        return remote(source, zr.at[s - 1], scr, s - 1, to_zp)

    def chain_left(s):
        source = u.at[nz - 3] if s == 2 else zl.at[s - 3]
        return remote(source, zl.at[s - 2], scl, s - 2, to_zm)

    greet((to_xp, to_xm, to_zp, to_zm))
    right(1).start()
    left(1).start()
    zg[0] = own[...]
    passed, scored = 0, 0
    for s in range(1, half + 1):
        right(s).wait_recv()
        if s < half:
            right(s + 1).start()
            left(s).wait_recv()
        if s < half - 1:
            left(s + 1).start()
        if s % 2 == 0:
            select(s // 2 - 1)
        if s % 2 and s >= 3:
            out_ring.pass_on(passed)
            passed += 1
        if s % 2 and s >= 5:
            score(scored)
            scored += 1
    while scored < groups - 1 and scored < passed:
        score(scored)
        scored += 1
    while passed < groups:
        out_ring.pass_on(passed)
        passed += 1
    while scored < groups:
        score(scored)
        scored += 1
    for g in reversed(range(groups)):
        give(g)
        if g < groups - 1:
            back_ring.pass_on(g + 1)
    summed = groups
    for s in range(1, half + 2):
        near = half + 1 - s
        while summed * GROUP > max(2 * near - 1, 0):
            summed -= 1
            if summed == 0:
                back_ring.pass_on(0)
            unselect(summed)
        if s > half:
            break
        if s > 1:
            chain_right(s - 1).wait_recv()
            zr[s - 2] = zr[s - 2] + u[2 * near]
        chain_right(s).start()
        if s > 2:
            chain_left(s - 1).wait_recv()
            zl[s - 3] = zl[s - 3] + u[2 * near - 1]
        if s > 1:
            chain_left(s).start()
    chain_right(half).wait_recv()
    chain_left(half).wait_recv()
    out[...] = u[0].astype(f32) + zr[half - 1].astype(f32) + zl[half - 2].astype(f32)
    for s in range(1, half + 1):
        right(s).wait_send()
        chain_right(s).wait_send()
        if s < half:
            left(s).wait_send()
        if s > 1:
            chain_left(s).wait_send()
    for g in range(groups):
        out_ring.drain(g)
        back_ring.drain(g)


def route_rows(own, label, nz, number):
    rows, wider = own.shape
    wide = label.shape[1]
    half, groups = nz // 2, nz // GROUP
    lot = GROUP * CAP * QBLOCK
    bf16 = jnp.bfloat16

    def over(width):
        low, high = halves(width)
        return [pltpu.VMEM((groups, lot, low.size), bf16), pltpu.VMEM((groups, lot, high.size), bf16)]

    return pl.pallas_call(
        functools.partial(route_kernel, nz),
        out_shape=jax.ShapeDtypeStruct((rows, wide), jnp.float32),
        in_specs=[pl.BlockSpec(memory_space=pltpu.VMEM)] * 2,
        out_specs=pl.BlockSpec(memory_space=pltpu.VMEM),
        scratch_shapes=[
            pltpu.VMEM((nz, rows, wider), bf16),
            pltpu.VMEM((groups, NX, lot, wider), bf16),
            pltpu.VMEM((groups, NX, lot, wider), bf16),
            pltpu.VMEM((groups, NX * lot, LBLOCK), bf16),
            pltpu.VMEM((groups, GROUP * rows, LANES), bf16),
            pltpu.VMEM((groups, NX, lot, wide), bf16),
            pltpu.VMEM((groups, NX, lot, wide), bf16),
            pltpu.VMEM((nz, rows, wide), bf16),
            pltpu.VMEM((half, rows, wide), bf16),
            pltpu.VMEM((half - 1, rows, wide), bf16),
            *over(wider),
            *over(wide),
            *pairs_of((half, half - 1, half, half - 1, *[groups] * 12)),
        ],
        compiler_params=pltpu.CompilerParams(
            collective_id=number, has_side_effects=True, vmem_limit_bytes=40 << 20
        ),
        cost_estimate=pl.CostEstimate(flops=0, bytes_accessed=150 << 20, transcendentals=0),
    )(own, label)


def groups_kernel(mine, out, near, hl, hr, far, nxt, prv, fl, fr, *sems):
    pair = [(sems[2 * i], sems[2 * i + 1]) for i in range(len(sems) // 2)]
    score, shl, shr, sfl, sfr = pair
    label = lax.axis_index("label")
    me = lax.axis_index("fsdp")
    y, core = me // CORES, me % CORES
    mate = 1 - core
    yp, ym, yo = (y + 1) % NY, (y + NY - 1) % NY, (y + 2) % NY
    to_mate, to_yp, to_ym = (label, y * CORES + mate), (label, yp * CORES + core), (label, ym * CORES + core)
    part = out.shape[0] // 2
    low, high = pl.ds(0, part), pl.ds(part, part)
    order = (yo, yp, ym, y)
    greet((to_mate, to_yp, to_ym))

    def across(i):
        return remote(mine.at[order[i] * CORES + mate], near.at[i], score, i, to_mate)

    def both(i):
        across(i).wait_recv()
        return mine[order[i] * CORES + core] + near[i]

    for i in range(NY):
        across(i).start()
    far[...] = both(0)
    far_right = remote(far.at[low], hl, shl, 0, to_yp)
    far_left = remote(far.at[high], hr, shr, 0, to_ym)
    far_right.start()
    far_left.start()
    nxt[...] = both(1)
    prv[...] = both(2)
    far_right.wait_recv()
    nxt[low] = nxt[low] + hl[...]
    near_right = remote(nxt, fl, sfl, 0, to_yp)
    near_right.start()
    far_left.wait_recv()
    prv[high] = prv[high] + hr[...]
    near_left = remote(prv, fr, sfr, 0, to_ym)
    near_left.start()
    here = both(3).astype(jnp.float32)
    near_right.wait_recv()
    here = here + fl[...].astype(jnp.float32)
    near_left.wait_recv()
    out[...] = here + fr[...].astype(jnp.float32)
    for copy in (far_right, far_left, near_right, near_left, *[across(i) for i in range(NY)]):
        copy.wait_send()


def sum_groups(mine, number):
    _, rows, wide = mine.shape
    kind = mine.dtype
    whole, piece = pltpu.VMEM((rows, wide), kind), pltpu.VMEM((rows // 2, wide), kind)
    return pl.pallas_call(
        groups_kernel,
        out_shape=jax.ShapeDtypeStruct((rows, wide), jnp.float32),
        in_specs=[pl.BlockSpec(memory_space=pltpu.VMEM)],
        out_specs=pl.BlockSpec(memory_space=pltpu.VMEM),
        scratch_shapes=[
            pltpu.VMEM((NY, rows, wide), kind),
            piece,
            piece,
            *[whole] * 5,
            *pairs_of((NY, 1, 1, 1, 1)),
        ],
        compiler_params=pltpu.CompilerParams(
            collective_id=number, has_side_effects=True, vmem_limit_bytes=24 << 20
        ),
        cost_estimate=pl.CostEstimate(flops=0, bytes_accessed=60 << 20, transcendentals=0),
    )(mine)


def shards(
    final_hidden, norm_gain, label_weights, active_blocks, positives, gate_pre, up_pre, down_weight
):
    owners = lax.axis_size("label")
    nz = owners // NX
    hidden_rows = final_hidden[0].astype(jnp.float32)
    query_count, width = hidden_rows.shape
    block_count = query_count // QBLOCK
    down_rows = with_layout_constraint(down_weight, Layout(major_to_minor=(0, 1)))
    down_full = lax.all_gather(down_rows, "fsdp", axis=0, tiled=True)
    inverse_rms = lax.rsqrt(
        jnp.mean(hidden_rows * hidden_rows, axis=1, keepdims=True) + norm_epsilon
    )
    normed = hidden_rows * inverse_rms
    embedded = (normed * norm_gain).astype(jnp.bfloat16)
    named = jnp.broadcast_to(
        active_blocks[0][:, None, :], (block_count, QBLOCK, ACTIVE)
    ).reshape(query_count, ACTIVE)
    codes = positives[0]
    marks = jnp.concatenate([named, codes // LBLOCK, codes % LBLOCK], axis=1)
    marks = jnp.pad(marks, ((0, 0), (0, LANES - marks.shape[1]))).astype(jnp.bfloat16)
    embed_grad = route_rows(
        jnp.concatenate([embedded, marks], axis=1), label_weights[0], nz, 0
    )
    scaled = norm_gain * embed_grad
    resid = inverse_rms * (scaled - normed * jnp.mean(normed * scaled, axis=1, keepdims=True))
    resid_bf = resid.astype(jnp.bfloat16)
    row_grads = gather_rows(resid_bf, nz, SPLIT, 2).reshape(owners * query_count, width)
    gate_full = gate_pre.astype(jnp.float32)
    up_full = up_pre.astype(jnp.float32)
    sigma = jax.nn.sigmoid(gate_full)
    ff_local = gate_pre.shape[2]
    hidden_act = (gate_full * sigma * up_full).astype(jnp.bfloat16)
    hidden_act = hidden_act.reshape(owners * query_count, ff_local)
    hidden_grad = jnp.dot(row_grads, down_full, preferred_element_type=jnp.float32)
    group_grad = lax.dot_general(
        row_grads, hidden_act, (((0,), (0,)), ((), ())), preferred_element_type=jnp.float32
    ).astype(jnp.bfloat16)
    down_grad = sum_groups(group_grad.reshape(NY * CORES, width // (NY * CORES), ff_local), 1)
    hidden_grad = hidden_grad.reshape(gate_pre.shape)
    up_grad = (hidden_grad * gate_full * sigma).astype(jnp.bfloat16)
    gate_grad = (hidden_grad * up_full * sigma * (1.0 + gate_full * (1.0 - sigma))).astype(
        jnp.bfloat16
    )
    return (resid_bf[None], down_grad, gate_grad, up_grad)


def solution(mesh):
    placed = (
        P("label", "fsdp", None),
        P(),
        P("label", None, None),
        P("label", "fsdp", None),
        P("label", "fsdp", None),
        P(None, "fsdp", "label"),
        P(None, "fsdp", "label"),
        P("fsdp", "label"),
    )
    return jax.shard_map(
        shards,
        mesh=mesh,
        in_specs=placed,
        out_specs=(
            P("label", "fsdp", None),
            P("fsdp", "label"),
            P(None, "fsdp", "label"),
            P(None, "fsdp", "label"),
        ),
        check_vma=False,
    )
```

```python
import functools

import jax
import jax.numpy as jnp
from jax import lax
from jax.experimental import pallas as pl
from jax.experimental.pallas import tpu as pltpu
from jax.sharding import PartitionSpec as P

LBLOCK = 128
ACTIVE = 8
POS = 8
QBLOCK = 2
NX = 4
NY = 4
CORES = 2
CAP = 2
GROUP = 4
CHUNK = 512
LANES = 128
LAG = 2

MESH = pl.DeviceIdType.MESH
norm_epsilon = 1e-06


def place(nz):
    me = lax.axis_index("label")
    other = lax.axis_index("fsdp")
    x = me // nz
    z = me % nz

    def device(px, pz):
        return (px * nz + pz, other)

    return x, z, device


def greet(devices):
    barrier = pltpu.get_barrier_semaphore()
    for target in devices:
        pl.semaphore_signal(barrier, inc=1, device_id=target, device_id_type=MESH)
    pl.semaphore_wait(barrier, len(devices))


def remote(src, dst, sems, slot, target):
    return pltpu.make_async_remote_copy(
        src_ref=src,
        dst_ref=dst,
        send_sem=sems[0].at[slot],
        recv_sem=sems[1].at[slot],
        device_id=target,
        device_id_type=MESH,
    )


def pairs_of(counts):
    return [pltpu.SemaphoreType.DMA((n,)) for n in counts for _ in range(2)]


def halves(wide):
    tiles = wide // LANES // 2 * LANES
    return pl.ds(0, tiles), pl.ds(tiles, wide - tiles)


class Ring:
    def __init__(self, here, to, sent, landed, sems):
        self.spots = ((here + 1) % NX, (here + NX - 1) % NX, (here + 2) % NX)
        self.here, self.to, self.sent, self.landed, self.sems = here, to, sent, landed, sems

    def copy(self, g, i):
        there = self.landed(g, self.here)
        return remote(self.sent(g, self.spots[i]), there, self.sems[i], g, self.to[i])

    def start(self, g):
        for i in (2, 0, 1):
            self.copy(g, i).start()

    def arrive(self, g):
        for i in range(3):
            self.copy(g, i).wait_recv()

    def drain(self, g):
        for i in range(3):
            self.copy(g, i).wait_send()


def chunks(wide, body):
    def one(i, carry):
        body(pl.ds(pl.multiple_of(i * CHUNK, CHUNK), CHUNK))
        return carry

    lax.fori_loop(0, wide // CHUNK, one, 0)


def route_kernel(
    nz, own, label, down, out, down_all, zg, sel, got, slope, picks, part, back, u, zr, zl, *sems
):
    pair = [(sems[2 * i], sems[2 * i + 1]) for i in range(len(sems) // 2)]
    szr, szl, scr, scl, sdn = pair[:5]
    half, groups = nz // 2, nz // GROUP
    wide = out.shape[1]
    rows = own.shape[0]
    taken = GROUP * rows
    slots = CAP * QBLOCK
    x, z, device = place(nz)
    xp, xm, xo = (x + 1) % NX, (x + NX - 1) % NX, (x + 2) % NX
    to_xp, to_xm = device(xp, z), device(xm, z)
    to_zp, to_zm = device(x, (z + 1) % nz), device(x, (z + nz - 1) % nz)
    f32, bf16 = jnp.float32, jnp.bfloat16
    to_xo = device(xo, z)
    near = (to_xp, to_xm, to_xo)
    out_ring = Ring(x, near, lambda g, d: sel.at[g, d], lambda g, d: got.at[g, d], pair[5:8])
    back_ring = Ring(x, near, lambda g, d: part.at[g, d], lambda g, d: back.at[g, d], pair[8:11])
    fsdp = lax.axis_index("fsdp")
    members = NY * CORES
    peers = [(lax.axis_index("label"), (fsdp + j) % members) for j in range(1, members)]
    sides, pieces = halves(own.shape[1]), halves(wide)

    def share(j):
        return remote(down, down_all.at[fsdp], sdn, j, peers[j])

    def right(s, c):
        source = own if s == 1 else zg.at[2 * s - 3]
        there = zg.at[2 * s - 1].at[:, sides[c]]
        return remote(source.at[:, sides[c]], there, szr, 2 * s - 2 + c, to_zp)

    def left(s, c):
        source = own if s == 1 else zg.at[2 * s - 2]
        there = zg.at[2 * s].at[:, sides[c]]
        return remote(source.at[:, sides[c]], there, szl, 2 * s - 2 + c, to_zm)

    def select(g):
        mine = pl.ds(GROUP * g, GROUP)
        marks = zg[mine, :, wide:].reshape(taken, LANES).astype(f32)
        row = lax.broadcasted_iota(jnp.int32, (taken, LANES), 0)
        col = lax.broadcasted_iota(jnp.int32, (taken, LANES), 1)
        owner = ((col // (GROUP * slots)) * nz + z).astype(f32)
        hit = marks[:, 0:1] == owner
        for k in range(1, ACTIVE):
            hit = hit | (marks[:, k : k + 1] == owner)
        before = lax.broadcasted_iota(jnp.int32, (taken, taken), 0)
        other = lax.broadcasted_iota(jnp.int32, (taken, taken), 1)
        earlier = (before // rows == other // rows) & (other // QBLOCK < before // QBLOCK)
        earlier = jnp.where(earlier & (other % QBLOCK == 0), 1.0, 0.0).astype(bf16)
        rank = jnp.dot(earlier, jnp.where(hit, 1.0, 0.0).astype(bf16), preferred_element_type=f32)
        slot = QBLOCK * rank + (row % QBLOCK).astype(f32)
        fits = (row // rows == (col // slots) % GROUP) & ((col % slots).astype(f32) == slot)
        pick = jnp.where(hit & fits, 1.0, 0.0).astype(bf16)
        picks[g] = pick
        wide_row = lax.broadcasted_iota(jnp.int32, (LANES, LANES), 0)
        wide_col = lax.broadcasted_iota(jnp.int32, (LANES, LANES), 1)
        unit = jnp.where(wide_row == wide_col, 1.0, 0.0).astype(bf16)
        turned = lax.dot_general(unit, pick, (((1,), (1,)), ((), ())), preferred_element_type=f32)
        turned = turned[: NX * GROUP * slots].astype(bf16)

        def place_columns(columns, count):
            block = zg[mine, :, columns].reshape(taken, count)
            made = jnp.dot(turned, block, preferred_element_type=f32).astype(bf16)
            sel[g, :, :, columns] = made.reshape(NX, GROUP * slots, count)

        chunks(wide, lambda columns: place_columns(columns, CHUNK))
        place_columns(pl.ds(wide, LANES), LANES)
        out_ring.start(g)
        got[g, x] = sel[g, x]

    def score(g):
        out_ring.arrive(g)
        count = NX * GROUP * slots
        block = got[g, :, :, :wide].reshape(count, wide)
        scores = lax.dot_general(
            block, label[...], (((1,), (1,)), ((), ())), preferred_element_type=f32
        )
        marks = got[g, :, :, wide:].reshape(count, LANES).astype(f32)
        me = (x * nz + z).astype(f32)
        spot = jnp.zeros((count, 1), f32)
        for k in range(1, ACTIVE):
            spot = spot + jnp.where(marks[:, k : k + 1] == me, float(k), 0.0)
        named = lax.broadcasted_iota(jnp.int32, (count, LBLOCK), 1).astype(f32)
        positive = jnp.zeros((count, LBLOCK), jnp.bool_)
        for p in range(ACTIVE, ACTIVE + POS):
            code = jnp.where(marks[:, p : p + 1] == spot, marks[:, p + POS : p + POS + 1], -1.0)
            positive = positive | (code == named)
        sign = jnp.where(positive, 1.0, -1.0)
        slope[g] = (-2.0 * sign * jnp.maximum(1.0 - sign * scores, 0.0)).astype(bf16)

    def give(g):
        steep = slope[g]

        def columns_of(columns):
            made = jnp.dot(steep, label[:, columns], preferred_element_type=f32).astype(bf16)
            part[g, :, :, columns] = made.reshape(NX, GROUP * slots, CHUNK)

        chunks(wide, columns_of)
        back_ring.start(g)
        back[g, x] = part[g, x]

    def unselect(g):
        back_ring.arrive(g)
        count = NX * GROUP * slots
        pick = picks[g][:, :count]

        def columns_of(columns):
            block = back[g, :, :, columns].reshape(count, CHUNK)
            made = jnp.dot(pick, block, preferred_element_type=f32).astype(bf16)
            u[pl.ds(GROUP * g, GROUP), :, columns] = made.reshape(GROUP, rows, CHUNK)

        chunks(wide, columns_of)

    def chain_right(s, c):
        source = u.at[nz - 1] if s == 1 else zr.at[s - 2]
        there = zr.at[s - 1].at[:, pieces[c]]
        return remote(source.at[:, pieces[c]], there, scr, 2 * s - 2 + c, to_zp)

    def chain_left(s, c):
        source = u.at[nz - 3] if s == 2 else zl.at[s - 3]
        there = zl.at[s - 2].at[:, pieces[c]]
        return remote(source.at[:, pieces[c]], there, scl, 2 * s - 4 + c, to_zm)

    greet((*near, to_zp, to_zm, *peers))
    for c in range(2):
        right(1, c).start()
        left(1, c).start()
    for j in range(members - 1):
        share(j).start()
    zg[0] = own[...]
    down_all[fsdp] = down[...]
    scored = 0
    for s in range(1, half + 1):
        for c in range(2):
            right(s, c).wait_recv()
            if s < half:
                right(s + 1, c).start()
                left(s, c).wait_recv()
            if s < half - 1:
                left(s + 1, c).start()
        if s % 2 == 0:
            select(s // 2 - 1)
        elif s >= 5:
            score(scored)
            scored += 1
    while scored < groups:
        score(scored)
        scored += 1
    for g in reversed(range(groups)):
        give(g)
    summed = groups
    for s in range(1, half + 2):
        far = half + 1 - s
        while summed * GROUP > max(2 * far - 1, 0):
            summed -= 1
            unselect(summed)
        if s > half:
            break
        for c, columns in enumerate(pieces):
            if s > 1:
                chain_right(s - 1, c).wait_recv()
                zr[s - 2, :, columns] = zr[s - 2, :, columns] + u[2 * far, :, columns]
            chain_right(s, c).start()
            if s > 2:
                chain_left(s - 1, c).wait_recv()
                zl[s - 3, :, columns] = zl[s - 3, :, columns] + u[2 * far - 1, :, columns]
            if s > 1:
                chain_left(s, c).start()
    for c in range(2):
        chain_right(half, c).wait_recv()
        chain_left(half, c).wait_recv()
    out[...] = u[0].astype(f32) + zr[half - 1].astype(f32) + zl[half - 2].astype(f32)
    for s in range(1, half + 1):
        for c in range(2):
            right(s, c).wait_send()
            chain_right(s, c).wait_send()
            if s < half:
                left(s, c).wait_send()
            if s > 1:
                chain_left(s, c).wait_send()
    for g in range(groups):
        out_ring.drain(g)
        back_ring.drain(g)
    for j in range(members - 1):
        share(j).wait()


def route_rows(own, label, down, nz, number):
    rows, wider = own.shape
    wide = label.shape[1]
    half, groups = nz // 2, nz // GROUP
    lot = GROUP * CAP * QBLOCK
    members = NY * CORES
    bf16 = jnp.bfloat16
    in_vmem = pl.BlockSpec(memory_space=pltpu.VMEM)
    return pl.pallas_call(
        functools.partial(route_kernel, nz),
        out_shape=(
            jax.ShapeDtypeStruct((rows, wide), jnp.float32),
            jax.ShapeDtypeStruct((members, *down.shape), down.dtype),
        ),
        in_specs=[in_vmem] * 3,
        out_specs=(in_vmem, in_vmem),
        scratch_shapes=[
            pltpu.VMEM((nz, rows, wider), bf16),
            pltpu.VMEM((groups, NX, lot, wider), bf16),
            pltpu.VMEM((groups, NX, lot, wider), bf16),
            pltpu.VMEM((groups, NX * lot, LBLOCK), bf16),
            pltpu.VMEM((groups, GROUP * rows, LANES), bf16),
            pltpu.VMEM((groups, NX, lot, wide), bf16),
            pltpu.VMEM((groups, NX, lot, wide), bf16),
            pltpu.VMEM((nz, rows, wide), bf16),
            pltpu.VMEM((half, rows, wide), bf16),
            pltpu.VMEM((half - 1, rows, wide), bf16),
            *pairs_of((nz, nz - 2, nz, nz - 2, members - 1, *[groups] * 6)),
        ],
        compiler_params=pltpu.CompilerParams(
            collective_id=number, has_side_effects=True, vmem_limit_bytes=40 << 20
        ),
        cost_estimate=pl.CostEstimate(flops=0, bytes_accessed=150 << 20, transcendentals=0),
    )(own, label, down)


def finish_kernel(nz, own, gate, up, down, down_out, gate_out, up_out, rows, hidden, acc, grads, near, far, nxt, prv, hl, hr, fl, fr, *sems):
    pair = [(sems[2 * i], sems[2 * i + 1]) for i in range(len(sems) // 2)]
    zar, zal, zbr, zbl, xal, xar, fal, fsr, xb, sac, shl, shr, sfl, sfr = pair
    half = nz // 2
    wide = rows.shape[-1]
    ff = gate.shape[-1]
    owned = wide // CORES
    x, z, device = place(nz)
    label = lax.axis_index("label")
    me = lax.axis_index("fsdp")
    y, core = me // CORES, me % CORES
    mate = 1 - core
    xp, xm, xo = (x + 1) % NX, (x + NX - 1) % NX, (x + 2) % NX
    to_xp, to_xm, to_xo = device(xp, z), device(xm, z), device(xo, z)
    to_zp, to_zm = device(x, (z + 1) % nz), device(x, (z + nz - 1) % nz)
    yp, ym, yo = (y + 1) % NY, (y + NY - 1) % NY, (y + 2) % NY
    to_mate, to_yp, to_ym = (label, y * CORES + mate), (label, yp * CORES + core), (label, ym * CORES + core)
    order = (yo, yp, ym, y)
    f32, bf16 = jnp.float32, jnp.bfloat16

    def cut(i):
        return (5 - i % 2) * wide // 7 // LANES * LANES

    def first(i):
        return pl.ds(0, cut(i))

    def second(i):
        return pl.ds(cut(i), wide - cut(i))

    def low(i):
        return pl.ds(0, cut(i) // 2 // LANES * LANES)

    def high(i):
        start = cut(i) // 2 // LANES * LANES
        return pl.ds(start, cut(i) - start)

    def block(i, px, o, columns):
        return rows.at[i, px, o, :, columns]

    def z_right(i, s):
        return remote(
            block(i, x, jnp.maximum(2 * s - 3, 0), first(i)), block(i, x, 2 * s - 1, first(i)), zar, i * half + s - 1, to_zp
        )

    def z_left(i, s):
        return remote(block(i, x, 2 * s - 2, first(i)), block(i, x, 2 * s, first(i)), zal, i * half + s - 1, to_zm)

    def wide_right(i, s):
        return remote(
            block(i, slice(None), jnp.maximum(2 * s - 3, 0), second(i)),
            block(i, slice(None), 2 * s - 1, second(i)),
            zbr,
            i * half + s - 1,
            to_zp,
        )

    def wide_left(i, s):
        return remote(
            block(i, slice(None), 2 * s - 2, second(i)),
            block(i, slice(None), jnp.minimum(2 * s, nz - 1), second(i)),
            zbl,
            i * half + s - 1,
            to_zm,
        )

    def along(i, s, count, px, columns, sem, target):
        start = 0 if isinstance(s, int) and s == 0 else 2 * s - 1
        there = rows.at[i, px, pl.ds(start, count), :, columns]
        return remote(there, there, sem, i * (half + 1) + s, target)

    def spread(i, s, count):
        along(i, s, count, x, first(i), xal, to_xp).start()
        along(i, s, count, x, first(i), xar, to_xm).start()

    def pass_on(i, s, count):
        along(i, s, count, xm, first(i), xal, to_xp).wait_recv()
        along(i, s, count, xm, low(i), fal, to_xp).start()
        along(i, s, count, xp, first(i), xar, to_xm).wait_recv()
        along(i, s, count, xp, high(i), fsr, to_xm).start()

    def passed(i, s, count):
        along(i, s, count, xo, low(i), fal, to_xp).wait_recv()
        along(i, s, count, xo, high(i), fsr, to_xm).wait_recv()

    def crossing(i, j):
        there = block(i, x, 0, second(i))
        return remote(there, there, xb, 3 * i + j, (to_xp, to_xm, to_xo)[j])

    def begin(i):
        rows[i, x, 0] = own[:, pl.ds(pl.multiple_of(order[i] * wide, LANES), wide)]
        for j in range(3):
            crossing(i, j).start()
        z_right(i, 1).start()
        z_left(i, 1).start()
        spread(i, 0, 1)

    def tick(i, s):
        @pl.when(s == 1)
        def _():
            for j in range(3):
                crossing(i, j).wait_recv()
            wide_right(i, 1).start()
            wide_left(i, 1).start()

        z_right(i, s).wait_recv()

        @pl.when(s < half)
        def _():
            z_right(i, s + 1).start()
            z_left(i, s).wait_recv()

        @pl.when(s < half - 1)
        def _():
            z_left(i, s + 1).start()

        @pl.when(s < half)
        def _():
            spread(i, s, 2)

        @pl.when(s == half)
        def _():
            spread(i, half, 1)

        wide_left(i, s).wait_recv()

        @pl.when(s < half)
        def _():
            wide_left(i, s + 1).start()
            wide_right(i, s).wait_recv()

        @pl.when(s < half - 1)
        def _():
            wide_right(i, s + 1).start()

        @pl.when(s == 1)
        def _():
            pass_on(i, 0, 1)

        @pl.when(s > 1)
        def _():
            pass_on(i, s - 1, 2)

    def z_of(o):
        return (z + nz + (1 - 2 * (o % 2)) * ((o + 1) // 2)) % nz

    def activate(o, carry):
        at = z_of(o)
        g, v = gate[:, at].astype(f32), up[:, at].astype(f32)
        hidden[:, o] = (g * (1.0 / (1.0 + jnp.exp(-g))) * v).astype(bf16)
        return carry

    count = NX * nz * own.shape[0]

    def across(i):
        there = pl.ds(pl.multiple_of(mate * owned, 16), owned)
        return remote(grads.at[i, there], near.at[i], sac, i, to_mate)

    def both(i):
        across(i).wait_recv()
        return grads[i, pl.ds(pl.multiple_of(core * owned, 16), owned)] + near[i]

    part = owned // 2
    top, bottom = pl.ds(0, part), pl.ds(part, part)

    def far_right():
        return remote(far.at[top], hl, shl, 0, to_yp)

    def far_left():
        return remote(far.at[bottom], hr, shr, 0, to_ym)

    def near_right():
        return remote(nxt, fl, sfl, 0, to_yp)

    def near_left():
        return remote(prv, fr, sfr, 0, to_ym)

    def weigh(i):
        passed(i, 0, 1)
        for s in range(1, half):
            passed(i, s, 2)
        passed(i, half, 1)
        acts = hidden[...].reshape(count, ff)

        def tile(c, carry):
            columns = pl.ds(pl.multiple_of(c * LANES, LANES), LANES)
            made = lax.dot_general(
                rows[i, :, :, :, columns].reshape(count, LANES),
                acts,
                (((0,), (0,)), ((), ())),
                preferred_element_type=f32,
            )
            grads[i, columns] = made.astype(bf16)
            return carry

        lax.fori_loop(0, wide // LANES, tile, 0)
        across(i).start()

    def project(i):
        weights = down[pl.ds(order[i] * CORES, CORES)].reshape(wide, ff)

        def quarter(q, carry):
            made = jnp.dot(rows[i, q].reshape(count // NX, wide), weights, preferred_element_type=f32)
            made = made.reshape(nz, own.shape[0], ff)
            acc[q] = made if i == 0 else acc[q] + made
            return carry

        lax.fori_loop(0, NX, quarter, 0)

    def onward(i):
        if i == 0:
            far[...] = both(0)
            far_right().start()
            far_left().start()
        elif i == 1:
            nxt[...] = both(1)
            far_right().wait_recv()
            nxt[top] = nxt[top] + hl[...]
            near_right().start()
        elif i == 2:
            prv[...] = both(2)
            far_left().wait_recv()
            prv[bottom] = prv[bottom] + hr[...]
            near_left().start()

    greet((to_xp, to_xm, to_xo, to_zp, to_zm, to_mate, to_yp, to_ym))
    begin(0)
    lax.fori_loop(0, nz, activate, 0)

    def wave(k, carry):
        for i in range(NY):
            s = k - LAG * i

            if i:

                @pl.when(s == 0)
                def _():
                    begin(i)

            @pl.when((s >= 1) & (s <= half))
            def _():
                tick(i, s)

            @pl.when(s == half + 1)
            def _():
                pass_on(i, half, 1)

        for i in range(NY):
            s = k - LAG * i

            @pl.when(s == half + 2)
            def _():
                weigh(i)

            @pl.when(s == half + 3)
            def _():
                project(i)

            if i < NY - 1:

                @pl.when(s == half + 4)
                def _():
                    onward(i)

        return carry

    lax.fori_loop(1, LAG * (NY - 1) + half + 4, wave, 0)

    def leave(o, carry):
        at = z_of(o)
        g, v, h = gate[:, at].astype(f32), up[:, at].astype(f32), acc[:, o]
        sigma = 1.0 / (1.0 + jnp.exp(-g))
        slope = h * sigma
        up_out[:, at] = (slope * g).astype(bf16)
        gate_out[:, at] = (slope * v * (1.0 + g * (1.0 - sigma))).astype(bf16)
        return carry

    lax.fori_loop(0, nz, leave, 0)
    here = both(NY - 1).astype(f32)
    near_right().wait_recv()
    here = here + fl[...].astype(f32)
    near_left().wait_recv()
    down_out[...] = here + fr[...].astype(f32)

    for copy in (far_right, far_left, near_right, near_left):
        copy().wait_send()
    for i in range(NY):
        across(i).wait_send()
        for j in range(3):
            crossing(i, j).wait_send()

        def sent(s, n):
            along(i, s, n, x, first(i), xal, to_xp).wait_send()
            along(i, s, n, x, first(i), xar, to_xm).wait_send()
            along(i, s, n, xm, low(i), fal, to_xp).wait_send()
            along(i, s, n, xp, high(i), fsr, to_xm).wait_send()

        def drain(s, carry):
            z_right(i, s).wait_send()
            wide_left(i, s).wait_send()

            @pl.when(s < half)
            def _():
                z_left(i, s).wait_send()
                wide_right(i, s).wait_send()
                sent(s, 2)

            return carry

        lax.fori_loop(1, half + 1, drain, 0)
        sent(0, 1)
        sent(half, 1)


def finish(own, gate, up, down, nz, number):
    rows, width = own.shape
    ff = gate.shape[-1]
    wide = width // NY
    half = nz // 2
    owned = wide // CORES
    bf16, f32 = jnp.bfloat16, jnp.float32
    in_vmem = pl.BlockSpec(memory_space=pltpu.VMEM)
    whole, piece = pltpu.VMEM((owned, ff), bf16), pltpu.VMEM((owned // 2, ff), bf16)
    shape = (NX, nz, rows, ff)
    return pl.pallas_call(
        functools.partial(finish_kernel, nz),
        out_shape=(
            jax.ShapeDtypeStruct((owned, ff), f32),
            jax.ShapeDtypeStruct(shape, bf16),
            jax.ShapeDtypeStruct(shape, bf16),
        ),
        in_specs=[in_vmem] * 4,
        out_specs=(in_vmem,) * 3,
        scratch_shapes=[
            pltpu.VMEM((NY, NX, nz, rows, wide), bf16),
            pltpu.VMEM(shape, bf16),
            pltpu.VMEM(shape, f32),
            pltpu.VMEM((NY, wide, ff), bf16),
            pltpu.VMEM((NY, owned, ff), bf16),
            whole,
            whole,
            whole,
            piece,
            piece,
            whole,
            whole,
            *pairs_of((*[NY * half] * 4, *[NY * (half + 1)] * 4, 3 * NY, NY, 1, 1, 1, 1)),
        ],
        compiler_params=pltpu.CompilerParams(
            collective_id=number, has_side_effects=True, vmem_limit_bytes=44 << 20
        ),
        cost_estimate=pl.CostEstimate(flops=0, bytes_accessed=150 << 20, transcendentals=0),
    )(own, gate.reshape(shape), up.reshape(shape), down)


def shards(
    final_hidden, norm_gain, label_weights, active_blocks, positives, gate_pre, up_pre, down_weight
):
    owners = lax.axis_size("label")
    nz = owners // NX
    hidden_rows = final_hidden[0].astype(jnp.float32)
    query_count, width = hidden_rows.shape
    block_count = query_count // QBLOCK
    inverse_rms = lax.rsqrt(
        jnp.mean(hidden_rows * hidden_rows, axis=1, keepdims=True) + norm_epsilon
    )
    normed = hidden_rows * inverse_rms
    embedded = (normed * norm_gain).astype(jnp.bfloat16)
    named = jnp.broadcast_to(
        active_blocks[0][:, None, :], (block_count, QBLOCK, ACTIVE)
    ).reshape(query_count, ACTIVE)
    codes = positives[0]
    marks = jnp.concatenate([named, codes // LBLOCK, codes % LBLOCK], axis=1)
    marks = jnp.pad(marks, ((0, 0), (0, LANES - marks.shape[1]))).astype(jnp.bfloat16)
    embed_grad, down_full = route_rows(
        jnp.concatenate([embedded, marks], axis=1), label_weights[0], down_weight, nz, 0
    )
    scaled = norm_gain * embed_grad
    resid = inverse_rms * (scaled - normed * jnp.mean(normed * scaled, axis=1, keepdims=True))
    resid_bf = resid.astype(jnp.bfloat16)
    down_grad, gate_grad, up_grad = finish(resid_bf, gate_pre, up_pre, down_full, nz, 1)
    return (
        resid_bf[None],
        down_grad,
        gate_grad.reshape(gate_pre.shape),
        up_grad.reshape(up_pre.shape),
    )


def solution(mesh):
    placed = (
        P("label", "fsdp", None),
        P(),
        P("label", None, None),
        P("label", "fsdp", None),
        P("label", "fsdp", None),
        P(None, "fsdp", "label"),
        P(None, "fsdp", "label"),
        P("fsdp", "label"),
    )
    return jax.shard_map(
        shards,
        mesh=mesh,
        in_specs=placed,
        out_specs=(
            P("label", "fsdp", None),
            P("fsdp", "label"),
            P(None, "fsdp", "label"),
            P(None, "fsdp", "label"),
        ),
        check_vma=False,
    )
```

```python
import functools

import jax
import jax.numpy as jnp
from jax import lax
from jax.experimental import pallas as pl
from jax.experimental.pallas import tpu as pltpu
from jax.sharding import PartitionSpec as P

LBLOCK = 128
ACTIVE = 8
POS = 8
QBLOCK = 2
NX = 4
NY = 4
CORES = 2
CAP = 2
GROUP = 4
CHUNK = 512
LANES = 128
LAG = 1

MESH = pl.DeviceIdType.MESH
norm_epsilon = 1e-06


def place(nz):
    me = lax.axis_index("label")
    other = lax.axis_index("fsdp")
    x = me // nz
    z = me % nz

    def device(px, pz):
        return (px * nz + pz, other)

    return x, z, device


def greet(devices):
    barrier = pltpu.get_barrier_semaphore()
    for target in devices:
        pl.semaphore_signal(barrier, inc=1, device_id=target, device_id_type=MESH)
    pl.semaphore_wait(barrier, len(devices))


def remote(src, dst, sems, slot, target, lot=None):
    return pltpu.make_async_remote_copy(
        src_ref=src,
        dst_ref=dst,
        send_sem=sems[0].at[slot if lot is None else lot],
        recv_sem=sems[1].at[slot],
        device_id=target,
        device_id_type=MESH,
    )


def pairs_of(counts):
    return [pltpu.SemaphoreType.DMA((n,)) for n in counts for _ in range(2)]


def halves(wide):
    tiles = wide // LANES // 2 * LANES
    return pl.ds(0, tiles), pl.ds(tiles, wide - tiles)


class Ring:
    def __init__(self, here, to, sent, landed, sems):
        self.spots = ((here + 1) % NX, (here + NX - 1) % NX, (here + 2) % NX)
        self.here, self.to, self.sent, self.landed, self.sems = here, to, sent, landed, sems

    def copy(self, g, i):
        there = self.landed(g, self.here)
        return remote(self.sent(g, self.spots[i]), there, self.sems[i], g, self.to[i], 0)

    def start(self, g):
        for i in (2, 0, 1):
            self.copy(g, i).start()

    def arrive(self, g):
        for i in range(3):
            self.copy(g, i).wait_recv()

    def drain(self, everything):
        for i in range(3):
            remote(everything, everything, self.sems[i], 0, self.to[i]).wait_send()


def chunks(wide, body):
    def one(i, carry):
        body(pl.ds(pl.multiple_of(i * CHUNK, CHUNK), CHUNK))
        return carry

    lax.fori_loop(0, wide // CHUNK, one, 0)


def route_kernel(
    nz, own, label, down, out, down_all, zg, sel, got, slope, picks, part, back, u, zr, zl, *sems
):
    pair = [(sems[2 * i], sems[2 * i + 1]) for i in range(len(sems) // 2)]
    szr, szl, scr, scl, sdn = pair[:5]
    half, groups = nz // 2, nz // GROUP
    wide = out.shape[1]
    rows = own.shape[0]
    taken = GROUP * rows
    slots = CAP * QBLOCK
    x, z, device = place(nz)
    xp, xm, xo = (x + 1) % NX, (x + NX - 1) % NX, (x + 2) % NX
    to_xp, to_xm = device(xp, z), device(xm, z)
    to_zp, to_zm = device(x, (z + 1) % nz), device(x, (z + nz - 1) % nz)
    f32, bf16 = jnp.float32, jnp.bfloat16
    to_xo = device(xo, z)
    near = (to_xp, to_xm, to_xo)
    out_ring = Ring(x, near, lambda g, d: sel.at[g, d], lambda g, d: got.at[g, d], pair[5:8])
    back_ring = Ring(x, near, lambda g, d: part.at[g, d], lambda g, d: back.at[g, d], pair[8:11])
    fsdp = lax.axis_index("fsdp")
    members = NY * CORES
    peers = [(lax.axis_index("label"), (fsdp + j) % members) for j in range(1, members)]
    sides, pieces = halves(own.shape[1]), halves(wide)

    def share(j):
        return remote(down, down_all.at[fsdp], sdn, j, peers[j])

    def right(s, c):
        source = own if s == 1 else zg.at[2 * s - 3]
        there = zg.at[2 * s - 1].at[:, sides[c]]
        return remote(source.at[:, sides[c]], there, szr, 2 * s - 2 + c, to_zp, 0)

    def left(s, c):
        source = own if s == 1 else zg.at[2 * s - 2]
        there = zg.at[2 * s].at[:, sides[c]]
        return remote(source.at[:, sides[c]], there, szl, 2 * s - 2 + c, to_zm, 0)

    def select(g):
        mine = pl.ds(GROUP * g, GROUP)
        marks = zg[mine, :, wide:].reshape(taken, LANES).astype(f32)
        row = lax.broadcasted_iota(jnp.int32, (taken, LANES), 0)
        col = lax.broadcasted_iota(jnp.int32, (taken, LANES), 1)
        owner = ((col // (GROUP * slots)) * nz + z).astype(f32)
        hit = marks[:, 0:1] == owner
        for k in range(1, ACTIVE):
            hit = hit | (marks[:, k : k + 1] == owner)
        before = lax.broadcasted_iota(jnp.int32, (taken, taken), 0)
        other = lax.broadcasted_iota(jnp.int32, (taken, taken), 1)
        earlier = (before // rows == other // rows) & (other // QBLOCK < before // QBLOCK)
        earlier = jnp.where(earlier & (other % QBLOCK == 0), 1.0, 0.0).astype(bf16)
        rank = jnp.dot(earlier, jnp.where(hit, 1.0, 0.0).astype(bf16), preferred_element_type=f32)
        slot = QBLOCK * rank + (row % QBLOCK).astype(f32)
        fits = (row // rows == (col // slots) % GROUP) & ((col % slots).astype(f32) == slot)
        pick = jnp.where(hit & fits, 1.0, 0.0).astype(bf16)
        picks[g] = pick
        wide_row = lax.broadcasted_iota(jnp.int32, (LANES, LANES), 0)
        wide_col = lax.broadcasted_iota(jnp.int32, (LANES, LANES), 1)
        unit = jnp.where(wide_row == wide_col, 1.0, 0.0).astype(bf16)
        turned = lax.dot_general(unit, pick, (((1,), (1,)), ((), ())), preferred_element_type=f32)
        turned = turned[: NX * GROUP * slots].astype(bf16)

        def place_columns(columns, count):
            block = zg[mine, :, columns].reshape(taken, count)
            made = jnp.dot(turned, block, preferred_element_type=f32).astype(bf16)
            sel[g, :, :, columns] = made.reshape(NX, GROUP * slots, count)

        chunks(wide, lambda columns: place_columns(columns, CHUNK))
        place_columns(pl.ds(wide, LANES), LANES)
        out_ring.start(g)
        got[g, x] = sel[g, x]

    def score(g):
        out_ring.arrive(g)
        count = NX * GROUP * slots
        block = got[g, :, :, :wide].reshape(count, wide)
        scores = lax.dot_general(
            block, label[...], (((1,), (1,)), ((), ())), preferred_element_type=f32
        )
        marks = got[g, :, :, wide:].reshape(count, LANES).astype(f32)
        me = (x * nz + z).astype(f32)
        spot = jnp.zeros((count, 1), f32)
        for k in range(1, ACTIVE):
            spot = spot + jnp.where(marks[:, k : k + 1] == me, float(k), 0.0)
        named = lax.broadcasted_iota(jnp.int32, (count, LBLOCK), 1).astype(f32)
        positive = jnp.zeros((count, LBLOCK), jnp.bool_)
        for p in range(ACTIVE, ACTIVE + POS):
            code = jnp.where(marks[:, p : p + 1] == spot, marks[:, p + POS : p + POS + 1], -1.0)
            positive = positive | (code == named)
        sign = jnp.where(positive, 1.0, -1.0)
        slope[g] = (-2.0 * sign * jnp.maximum(1.0 - sign * scores, 0.0)).astype(bf16)

    def give(g):
        steep = slope[g]

        def columns_of(columns):
            made = jnp.dot(steep, label[:, columns], preferred_element_type=f32).astype(bf16)
            part[g, :, :, columns] = made.reshape(NX, GROUP * slots, CHUNK)

        chunks(wide, columns_of)
        back_ring.start(g)
        back[g, x] = part[g, x]

    def unselect(g):
        back_ring.arrive(g)
        count = NX * GROUP * slots
        pick = picks[g][:, :count]

        def columns_of(columns):
            block = back[g, :, :, columns].reshape(count, CHUNK)
            made = jnp.dot(pick, block, preferred_element_type=f32).astype(bf16)
            u[pl.ds(GROUP * g, GROUP), :, columns] = made.reshape(GROUP, rows, CHUNK)

        chunks(wide, columns_of)

    def chain_right(s, c):
        source = u.at[nz - 1] if s == 1 else zr.at[s - 2]
        there = zr.at[s - 1].at[:, pieces[c]]
        return remote(source.at[:, pieces[c]], there, scr, 2 * s - 2 + c, to_zp, 0)

    def chain_left(s, c):
        source = u.at[nz - 3] if s == 2 else zl.at[s - 3]
        there = zl.at[s - 2].at[:, pieces[c]]
        return remote(source.at[:, pieces[c]], there, scl, 2 * s - 4 + c, to_zm, 0)

    greet((*near, to_zp, to_zm, *peers))
    for c in range(2):
        right(1, c).start()
        left(1, c).start()
    for j in range(members - 1):
        share(j).start()
    zg[0] = own[...]
    down_all[fsdp] = down[...]
    scored = 0
    for s in range(1, half + 1):
        for c in range(2):
            right(s, c).wait_recv()
            if s < half:
                right(s + 1, c).start()
                left(s, c).wait_recv()
            if s < half - 1:
                left(s + 1, c).start()
        if s % 2 == 0:
            select(s // 2 - 1)
        elif s >= 5:
            score(scored)
            scored += 1
    while scored < groups:
        score(scored)
        scored += 1
    for g in reversed(range(groups)):
        give(g)
    summed = groups
    for s in range(1, half + 2):
        far = half + 1 - s
        while summed * GROUP > max(2 * far - 1, 0):
            summed -= 1
            unselect(summed)
        if s > half:
            break
        for c, columns in enumerate(pieces):
            if s > 1:
                chain_right(s - 1, c).wait_recv()
                zr[s - 2, :, columns] = zr[s - 2, :, columns] + u[2 * far, :, columns]
            chain_right(s, c).start()
            if s > 2:
                chain_left(s - 1, c).wait_recv()
                zl[s - 3, :, columns] = zl[s - 3, :, columns] + u[2 * far - 1, :, columns]
            if s > 1:
                chain_left(s, c).start()
    for c in range(2):
        chain_right(half, c).wait_recv()
        chain_left(half, c).wait_recv()
    out[...] = u[0].astype(f32) + zr[half - 1].astype(f32) + zl[half - 2].astype(f32)
    for sem, there in (
        (szr, zg.at[pl.ds(0, half)]),
        (szl, zg.at[pl.ds(0, half - 1)]),
        (scr, zr),
        (scl, zl),
    ):
        remote(there, there, sem, 0, to_zp).wait_send()
    out_ring.drain(sel.at[:, x])
    back_ring.drain(part.at[:, x])
    for j in range(members - 1):
        share(j).wait()


def route_rows(own, label, down, nz, number):
    rows, wider = own.shape
    wide = label.shape[1]
    half, groups = nz // 2, nz // GROUP
    lot = GROUP * CAP * QBLOCK
    members = NY * CORES
    bf16 = jnp.bfloat16
    in_vmem = pl.BlockSpec(memory_space=pltpu.VMEM)
    return pl.pallas_call(
        functools.partial(route_kernel, nz),
        out_shape=(
            jax.ShapeDtypeStruct((rows, wide), jnp.float32),
            jax.ShapeDtypeStruct((members, *down.shape), down.dtype),
        ),
        in_specs=[in_vmem] * 3,
        out_specs=(in_vmem, in_vmem),
        scratch_shapes=[
            pltpu.VMEM((nz, rows, wider), bf16),
            pltpu.VMEM((groups, NX, lot, wider), bf16),
            pltpu.VMEM((groups, NX, lot, wider), bf16),
            pltpu.VMEM((groups, NX * lot, LBLOCK), bf16),
            pltpu.VMEM((groups, GROUP * rows, LANES), bf16),
            pltpu.VMEM((groups, NX, lot, wide), bf16),
            pltpu.VMEM((groups, NX, lot, wide), bf16),
            pltpu.VMEM((nz, rows, wide), bf16),
            pltpu.VMEM((half, rows, wide), bf16),
            pltpu.VMEM((half - 1, rows, wide), bf16),
            *pairs_of((nz, nz - 2, nz, nz - 2, members - 1, *[groups] * 6)),
        ],
        compiler_params=pltpu.CompilerParams(
            collective_id=number, has_side_effects=True, vmem_limit_bytes=40 << 20
        ),
        cost_estimate=pl.CostEstimate(flops=0, bytes_accessed=150 << 20, transcendentals=0),
    )(own, label, down)


def finish_kernel(nz, own, gate, up, down, down_out, gate_out, up_out, rows, hidden, acc, grads, near, far, nxt, prv, hl, hr, fl, fr, *sems):
    pair = [(sems[2 * i], sems[2 * i + 1]) for i in range(len(sems) // 2)]
    zar, zal, zbr, zbl, xal, xar, fal, fsr, xb, sac, shl, shr, sfl, sfr = pair
    half = nz // 2
    wide = rows.shape[-1]
    ff = gate.shape[-1]
    owned = wide // CORES
    x, z, device = place(nz)
    label = lax.axis_index("label")
    me = lax.axis_index("fsdp")
    y, core = me // CORES, me % CORES
    mate = 1 - core
    xp, xm, xo = (x + 1) % NX, (x + NX - 1) % NX, (x + 2) % NX
    to_xp, to_xm, to_xo = device(xp, z), device(xm, z), device(xo, z)
    to_zp, to_zm = device(x, (z + 1) % nz), device(x, (z + nz - 1) % nz)
    yp, ym, yo = (y + 1) % NY, (y + NY - 1) % NY, (y + 2) % NY
    to_mate, to_yp, to_ym = (label, y * CORES + mate), (label, yp * CORES + core), (label, ym * CORES + core)
    order = (yo, yp, ym, y)
    f32, bf16 = jnp.float32, jnp.bfloat16

    def cut(i):
        return (5 - i % 2) * wide // 7 // LANES * LANES

    def first(i):
        return pl.ds(0, cut(i))

    def second(i):
        return pl.ds(cut(i), wide - cut(i))

    def low(i):
        return pl.ds(0, cut(i) // 2 // LANES * LANES)

    def high(i):
        start = cut(i) // 2 // LANES * LANES
        return pl.ds(start, cut(i) - start)

    def block(i, px, o, columns):
        return rows.at[i, px, o, :, columns]

    def z_right(i, s):
        return remote(
            block(i, x, jnp.maximum(2 * s - 3, 0), first(i)), block(i, x, 2 * s - 1, first(i)), zar, i * half + s - 1, to_zp, i
        )

    def z_left(i, s):
        return remote(block(i, x, 2 * s - 2, first(i)), block(i, x, 2 * s, first(i)), zal, i * half + s - 1, to_zm, i)

    def wide_right(i, s):
        return remote(
            block(i, slice(None), jnp.maximum(2 * s - 3, 0), second(i)),
            block(i, slice(None), 2 * s - 1, second(i)),
            zbr,
            i * half + s - 1,
            to_zp,
            i,
        )

    def wide_left(i, s):
        return remote(
            block(i, slice(None), 2 * s - 2, second(i)),
            block(i, slice(None), jnp.minimum(2 * s, nz - 1), second(i)),
            zbl,
            i * half + s - 1,
            to_zm,
            i,
        )

    def along(i, s, count, px, columns, sem, target, slot=None):
        start = 0 if isinstance(s, int) and s == 0 else 2 * s - 1
        there = rows.at[i, px, pl.ds(start, count), :, columns]
        return remote(there, there, sem, i * (half + 1) + s if slot is None else slot, target, i)

    def spread(i, s, count):
        along(i, s, count, x, first(i), xal, to_xp).start()
        along(i, s, count, x, first(i), xar, to_xm).start()

    def pass_on(i, s, count):
        along(i, s, count, xm, first(i), xal, to_xp).wait_recv()
        along(i, s, count, xm, low(i), fal, to_xp, i).start()
        along(i, s, count, xp, first(i), xar, to_xm).wait_recv()
        along(i, s, count, xp, high(i), fsr, to_xm, i).start()

    def passed(i):
        along(i, 0, nz, xo, low(i), fal, to_xp, i).wait_recv()
        along(i, 0, nz, xo, high(i), fsr, to_xm, i).wait_recv()

    def crossing(i, j):
        there = block(i, x, 0, second(i))
        return remote(there, there, xb, 3 * i + j, (to_xp, to_xm, to_xo)[j], i)

    def begin(i):
        rows[i, x, 0] = own[:, pl.ds(pl.multiple_of(order[i] * wide, LANES), wide)]
        for j in range(3):
            crossing(i, j).start()
        z_right(i, 1).start()
        z_left(i, 1).start()
        spread(i, 0, 1)

    def tick(i, s):
        @pl.when(s == 1)
        def _():
            for j in range(3):
                crossing(i, j).wait_recv()
            wide_right(i, 1).start()
            wide_left(i, 1).start()

        z_right(i, s).wait_recv()

        @pl.when(s < half)
        def _():
            z_right(i, s + 1).start()
            z_left(i, s).wait_recv()

        @pl.when(s < half - 1)
        def _():
            z_left(i, s + 1).start()

        @pl.when(s < half)
        def _():
            spread(i, s, 2)

        @pl.when(s == half)
        def _():
            spread(i, half, 1)

    def tock(i, s):
        wide_left(i, s).wait_recv()

        @pl.when(s < half)
        def _():
            wide_left(i, s + 1).start()
            wide_right(i, s).wait_recv()

        @pl.when(s < half - 1)
        def _():
            wide_right(i, s + 1).start()

    def tack(i, s):
        @pl.when(s == 1)
        def _():
            pass_on(i, 0, 1)

        @pl.when(s > 1)
        def _():
            pass_on(i, s - 1, 2)

    def z_of(o):
        return (z + nz + (1 - 2 * (o % 2)) * ((o + 1) // 2)) % nz

    def activate(o, carry):
        at = z_of(o)
        g, v = gate[:, at].astype(f32), up[:, at].astype(f32)
        hidden[:, o] = (g * (1.0 / (1.0 + jnp.exp(-g))) * v).astype(bf16)
        return carry

    count = NX * nz * own.shape[0]

    def across(i):
        there = pl.ds(pl.multiple_of(mate * owned, 16), owned)
        return remote(grads.at[i, there], near.at[i], sac, i, to_mate)

    def both(i):
        across(i).wait_recv()
        return grads[i, pl.ds(pl.multiple_of(core * owned, 16), owned)] + near[i]

    part = owned // 2
    top, bottom = pl.ds(0, part), pl.ds(part, part)

    def far_right():
        return remote(far.at[top], hl, shl, 0, to_yp)

    def far_left():
        return remote(far.at[bottom], hr, shr, 0, to_ym)

    def near_right():
        return remote(nxt, fl, sfl, 0, to_yp)

    def near_left():
        return remote(prv, fr, sfr, 0, to_ym)

    def weigh(i):
        passed(i)
        acts = hidden[...].reshape(count, ff)

        made = lax.dot_general(
            rows[i].reshape(count, wide), acts, (((0,), (0,)), ((), ())), preferred_element_type=f32
        )
        grads[i] = made.astype(bf16)
        across(i).start()

    def project(i):
        weights = down[pl.ds(order[i] * CORES, CORES)].reshape(wide, ff)

        def quarter(q, carry):
            made = jnp.dot(rows[i, q].reshape(count // NX, wide), weights, preferred_element_type=f32)
            made = made.reshape(nz, own.shape[0], ff)
            acc[q] = made if i == 0 else acc[q] + made
            return carry

        lax.fori_loop(0, NX, quarter, 0)

    def onward(i):
        if i == 0:
            far[...] = both(0)
            far_right().start()
            far_left().start()
        elif i == 1:
            nxt[...] = both(1)
            far_right().wait_recv()
            nxt[top] = nxt[top] + hl[...]
            near_right().start()
        elif i == 2:
            prv[...] = both(2)
            far_left().wait_recv()
            prv[bottom] = prv[bottom] + hr[...]
            near_left().start()

    greet((to_xp, to_xm, to_xo, to_zp, to_zm, to_mate, to_yp, to_ym))
    begin(0)
    lax.fori_loop(0, nz, activate, 0)

    def wave(k, carry):
        for i in range(NY):
            s = k - LAG * i

            if i:

                @pl.when(s == 0)
                def _():
                    begin(i)

            @pl.when((s >= 1) & (s <= half))
            def _():
                tick(i, s)

        for i in range(NY):
            s = k - LAG * i

            @pl.when((s >= 1) & (s <= half))
            def _():
                tock(i, s)

        for i in range(NY):
            s = k - LAG * i

            @pl.when((s >= 1) & (s <= half))
            def _():
                tack(i, s)

            @pl.when(s == half + 1)
            def _():
                pass_on(i, half, 1)

        for i in range(NY - 1):

            @pl.when(k - LAG * i == half + 3)
            def _():
                onward(i)

        for i in range(NY):

            @pl.when(k - LAG * i == half + 2)
            def _():
                weigh(i)

        for i in range(NY):

            @pl.when(k - LAG * i == half + 3)
            def _():
                project(i)

        return carry

    lax.fori_loop(1, LAG * (NY - 1) + half + 4, wave, 0)

    def leave(o, carry):
        at = z_of(o)
        g, v, h = gate[:, at].astype(f32), up[:, at].astype(f32), acc[:, o]
        sigma = 1.0 / (1.0 + jnp.exp(-g))
        slope = h * sigma
        up_out[:, at] = (slope * g).astype(bf16)
        gate_out[:, at] = (slope * v * (1.0 + g * (1.0 - sigma))).astype(bf16)
        return carry

    lax.fori_loop(0, nz, leave, 0)
    here = both(NY - 1).astype(f32)
    near_right().wait_recv()
    here = here + fl[...].astype(f32)
    near_left().wait_recv()
    down_out[...] = here + fr[...].astype(f32)

    for copy in (far_right, far_left, near_right, near_left):
        copy().wait_send()
    for i in range(NY):
        across(i).wait_send()
        three = rows.at[i, pl.ds(0, 3), 0, :, second(i)]
        remote(three, three, xb, 3 * i, to_xp, i).wait_send()
        for sem, n, columns in ((zar, half, first(i)), (zal, half - 1, first(i)), (xal, nz, first(i)), (xar, nz, first(i))):
            along(i, 0, n, x, columns, sem, to_xp).wait_send()
        along(i, 0, nz, xm, low(i), fal, to_xp, i).wait_send()
        along(i, 0, nz, xp, high(i), fsr, to_xm, i).wait_send()
        for sem, n in ((zbr, half - 1), (zbl, half)):
            along(i, 0, n, slice(None), second(i), sem, to_xp, i).wait_send()


def finish(own, gate, up, down, nz, number):
    rows, width = own.shape
    ff = gate.shape[-1]
    wide = width // NY
    half = nz // 2
    owned = wide // CORES
    bf16, f32 = jnp.bfloat16, jnp.float32
    in_vmem = pl.BlockSpec(memory_space=pltpu.VMEM)
    whole, piece = pltpu.VMEM((owned, ff), bf16), pltpu.VMEM((owned // 2, ff), bf16)
    shape = (NX, nz, rows, ff)
    return pl.pallas_call(
        functools.partial(finish_kernel, nz),
        out_shape=(
            jax.ShapeDtypeStruct((owned, ff), f32),
            jax.ShapeDtypeStruct(shape, bf16),
            jax.ShapeDtypeStruct(shape, bf16),
        ),
        in_specs=[in_vmem] * 4,
        out_specs=(in_vmem,) * 3,
        scratch_shapes=[
            pltpu.VMEM((NY, NX, nz, rows, wide), bf16),
            pltpu.VMEM(shape, bf16),
            pltpu.VMEM(shape, f32),
            pltpu.VMEM((NY, wide, ff), bf16),
            pltpu.VMEM((NY, owned, ff), bf16),
            whole,
            whole,
            whole,
            piece,
            piece,
            whole,
            whole,
            *pairs_of((*[NY * half] * 4, NY * (half + 1), NY * (half + 1), NY, NY, 3 * NY, NY, 1, 1, 1, 1)),
        ],
        compiler_params=pltpu.CompilerParams(
            collective_id=number, has_side_effects=True, vmem_limit_bytes=44 << 20
        ),
        cost_estimate=pl.CostEstimate(flops=0, bytes_accessed=150 << 20, transcendentals=0),
    )(own, gate.reshape(shape), up.reshape(shape), down)


def shards(
    final_hidden, norm_gain, label_weights, active_blocks, positives, gate_pre, up_pre, down_weight
):
    owners = lax.axis_size("label")
    nz = owners // NX
    hidden_rows = final_hidden[0].astype(jnp.float32)
    query_count, width = hidden_rows.shape
    block_count = query_count // QBLOCK
    inverse_rms = lax.rsqrt(
        jnp.mean(hidden_rows * hidden_rows, axis=1, keepdims=True) + norm_epsilon
    )
    normed = hidden_rows * inverse_rms
    embedded = (normed * norm_gain).astype(jnp.bfloat16)
    named = jnp.broadcast_to(
        active_blocks[0][:, None, :], (block_count, QBLOCK, ACTIVE)
    ).reshape(query_count, ACTIVE)
    codes = positives[0]
    marks = jnp.concatenate([named, codes // LBLOCK, codes % LBLOCK], axis=1)
    marks = jnp.pad(marks, ((0, 0), (0, LANES - marks.shape[1]))).astype(jnp.bfloat16)
    embed_grad, down_full = route_rows(
        jnp.concatenate([embedded, marks], axis=1), label_weights[0], down_weight, nz, 0
    )
    scaled = norm_gain * embed_grad
    resid = inverse_rms * (scaled - normed * jnp.mean(normed * scaled, axis=1, keepdims=True))
    resid_bf = resid.astype(jnp.bfloat16)
    down_grad, gate_grad, up_grad = finish(resid_bf, gate_pre, up_pre, down_full, nz, 1)
    return (
        resid_bf[None],
        down_grad,
        gate_grad.reshape(gate_pre.shape),
        up_grad.reshape(up_pre.shape),
    )


def solution(mesh):
    placed = (
        P("label", "fsdp", None),
        P(),
        P("label", None, None),
        P("label", "fsdp", None),
        P("label", "fsdp", None),
        P(None, "fsdp", "label"),
        P(None, "fsdp", "label"),
        P("fsdp", "label"),
    )
    return jax.shard_map(
        shards,
        mesh=mesh,
        in_specs=placed,
        out_specs=(
            P("label", "fsdp", None),
            P("fsdp", "label"),
            P(None, "fsdp", "label"),
            P(None, "fsdp", "label"),
        ),
        check_vma=False,
    )
```
